32 devices in a mesh: dp: 4 (over y, core), owner: 8 (over z, x).
Axes of the slice: x: 2, y: 2, z: 4, core: 2. Of those that a mesh axis runs over, the one named last changes fastest.
Arguments:
- embeddings: bfloat16 [131072, 1024], P(('dp', 'owner')), may hold values from -40 to 40, as said below
- cluster_ids: int32 [131072, 1], P(('dp', 'owner')), may hold values from 0 to 63; in each aligned block of 4096 rows (0 to 4095, 4096 to 8191, ...) at most 128 rows name the same one
- noise: bfloat16 [131072, 256], P(('dp', 'owner')), may hold values from -3 to 3
- start_basis: float32 [1024, 256], replicated, may hold values from -0.1875 to 0.1875
Outputs:
- routed: bfloat16 [4, 64, 8, 128, 256], P('dp', 'owner')
The draws below stay inside these ranges and needn't reach their ends.
Inputs may be any that keep to these rules, and one draw needn't show every extreme that they name: `embeddings`: entries are of order one around a column mean. `cluster_ids`: no cluster holds more than 128 rows of one device, and some cluster holds exactly 128 rows of some device.
All inputs are finite; a program needn't handle non-finite values.
Results may differ from the reference program's by a relative error of at most 0.0046.
Values may be sent and summed in bfloat16 or wider, within the bound.
No kernel may reach another device: no remote copies, remote signals or barrier semaphores. Data moves between devices by JAX's collectives and lax.ppermute only.
A program may use at most 128 MiB of HBM per device.

```python
import math
import jax
import jax.numpy as jnp
import numpy as np
from jax import lax

D = 1024
K = 256
ROWS_DEV = 4096
ROWS = 131072
CLUSTERS = 64
MOST = 128
N_DP = 4
N_OWNER = 8


def draw_embeddings(key, part):
    key_centre, key_spread, key_rough = jax.random.split(key, 3)
    centre = 0.5 * jax.random.normal(key_centre, (D,), jnp.float32)
    spread = jnp.exp(jax.random.uniform(key_spread, (D,), jnp.float32, math.log(0.4), math.log(2.5)))
    rough = jax.random.normal(key_rough, (ROWS, D), jnp.float32)
    values = centre[None, :] + spread[None, :] * rough
    return values.astype(jnp.bfloat16)


def shard_levels(rng, dims, shards, smallest, largest):
    def one(position, parts):
        heights = jax.random.uniform(jax.random.fold_in(jax.random.fold_in(rng, 6), position), (parts,), jnp.float32, smallest / len(shards), largest / len(shards))
        return jnp.repeat(jnp.exp(heights), dims[position] // parts).reshape((-1,) + (1,) * (len(dims) - position - 1))

    factor_of = one(*shards[0])
    for cut in shards[1:]:
        factor_of = factor_of * one(*cut)
    return factor_of


def assign_block(rng, own, number, rows, number_of, top, limit, skew):
    order = jax.random.permutation(rng, number_of)
    crowded, common = portions_of(number_of, rows * top, limit, skew, True), portions_of(number_of, rows * top, limit, skew, False)
    places = jnp.arange(number_of)

    def named(lengths, turn):
        used = int((lengths > 0).sum())
        fixed = max(1, used // 4)
        passed = fixed + (places - fixed + turn * (used - fixed)) % max(1, number_of - fixed)
        return jnp.zeros((number_of,), jnp.int32).at[order[jnp.where(places < fixed, places, passed)]].set(jnp.asarray(lengths, jnp.int32))

    lengths = jnp.where(number % 4 == 0, named(crowded, number // 4), named(common, number - number // 4 - 1))
    mixed = jax.random.permutation(jax.random.fold_in(own, 3), number_of)
    source_of, sink = mixed[0:number_of // 2 * 2:2], mixed[1:number_of // 2 * 2:2]
    slack = jnp.minimum(lengths[source_of] - 1, limit - lengths[sink]) // 2
    slack = jnp.where((source_of == order[0]) | (sink == order[0]) | (lengths[sink] == 0), 0, jnp.maximum(slack, 0))
    passed = jax.random.randint(jax.random.fold_in(own, 4), (number_of // 2,), 0, 1 << 20) % (slack + 1)
    lengths = lengths.at[source_of].add(-passed).at[sink].add(passed)
    labels = jnp.searchsorted(jnp.cumsum(lengths), jnp.arange(rows * top), side="right").astype(jnp.int32)
    table = labels.reshape(top, rows).T
    table = table[jax.random.permutation(jax.random.fold_in(own, 1), rows)]
    turn = jax.random.randint(jax.random.fold_in(own, 2), (rows, 1), 0, top)
    return jnp.take_along_axis(table, (jnp.arange(top)[None, :] + turn) % top, axis=1)


def portions_of(amount, total, bound, slope, full):
    portions = [(1 << 20) // math.isqrt(rank ** slope) + 1 for rank in range(1, amount + 1)]
    largest = bound if full else min(bound, max(-(-total // amount), total * portions[0] // sum(portions)))
    least = 1 if total - largest >= amount - 1 else 0
    counts, rest = [largest] + [least] * (amount - 1), total - largest - least * (amount - 1)
    while rest > 0:
        free = [i for i in range(1, amount) if counts[i] < largest] or [i for i in range(1, amount) if counts[i] < bound]
        mass, left = sum([portions[i] for i in free]), rest
        for i in free:
            more = min(bound - counts[i], max(1, left * portions[i] // mass), rest)
            counts[i] = counts[i] + more
            rest = rest - more
    return np.array(counts)


def bell_draw(key, dims, scale, limit, shards=(), held_as=jnp.bfloat16):
    values = scale * jax.random.normal(key, dims, jnp.float32)
    if shards:
        values = values * shard_levels(key, dims, shards, -0.22, 0.18)
    return jnp.clip(values, -limit, limit).astype(held_as)


def setup_inputs(seed: int = 0) -> dict:
    key_of = jax.random.split(jax.random.key(seed), 5)
    embeddings = draw_embeddings(jax.random.fold_in(key_of[4], 71), 0)
    cluster_ids_keys = jax.random.split(jax.random.fold_in(key_of[1], 1), ROWS // ROWS_DEV)
    cluster_ids_turns = jax.random.permutation(jax.random.fold_in(key_of[1], 3), ROWS // ROWS_DEV)
    cluster_ids = jax.vmap(lambda own, number: assign_block(jax.random.fold_in(key_of[1], 2), own, number, ROWS_DEV, CLUSTERS, 1, MOST, 2))(cluster_ids_keys, cluster_ids_turns).reshape((ROWS, 1))
    noise = bell_draw(key_of[2], (ROWS, K), 0.5, 3.0, ((0, 32),))
    start_basis = bell_draw(key_of[3], (D, K), D ** -0.5, 0.1875, (), jnp.float32)
    return {"embeddings": embeddings, "cluster_ids": cluster_ids, "noise": noise, "start_basis": start_basis}


def reference(embeddings, cluster_ids, noise, start_basis):
    highest = lax.Precision.HIGHEST
    device_count = N_DP * N_OWNER
    device_rows = embeddings.reshape(device_count, ROWS_DEV, D)

    def add_block(running, rows_here):
        second, column_sum = running
        second = second + lax.dot_general(rows_here.astype(jnp.float32), rows_here.astype(jnp.float32), (((0,), (0,)), ((), ())), preferred_element_type=jnp.float32)
        column_sum = column_sum + lax.optimization_barrier(jnp.sum(rows_here, axis=0, dtype=jnp.float32))
        return ((second, column_sum), None)
    init = (jnp.zeros((D, D), jnp.float32), jnp.zeros((D,), jnp.float32))
    (second, column_sum), _ = lax.scan(add_block, init, device_rows)
    mean_vec = column_sum / ROWS
    covariance = second / ROWS - jnp.outer(mean_vec, mean_vec)
    image_rows = jnp.dot(covariance, start_basis, precision=highest)
    gram_matrix = jnp.dot(image_rows.T, image_rows, precision=highest)
    lower_factor = jnp.linalg.cholesky(gram_matrix)
    basis_full = lax.linalg.triangular_solve(lower_factor, image_rows, left_side=False, lower=True, transpose_a=True)
    curved = jnp.dot(covariance, basis_full, precision=highest)
    eigen_vals = lax.optimization_barrier(jnp.sum(basis_full * curved, axis=0))
    signed = math.sqrt(D) * lax.optimization_barrier(jnp.sum(basis_full, axis=0))
    flip_sign = signed / jnp.maximum(jnp.abs(signed), 1.0)
    whiten = (basis_full * (flip_sign / jnp.sqrt(eigen_vals + 1e-06))).astype(jnp.bfloat16)
    offset = jnp.dot(mean_vec, whiten.astype(jnp.float32), precision=highest)
    device_ids = cluster_ids.reshape(device_count, ROWS_DEV)
    device_noise = noise.reshape(device_count, ROWS_DEV, K)

    def place(packed_in):
        rows_here, ids_here, noise_here = packed_in
        projected = (jnp.dot(rows_here.astype(jnp.float32), whiten.astype(jnp.float32), preferred_element_type=jnp.float32) - offset + noise_here.astype(jnp.float32)).astype(jnp.bfloat16)
        onehot = (ids_here[:, None] == jnp.arange(CLUSTERS, dtype=jnp.int32)[None, :]).astype(jnp.int32)
        before = jnp.cumsum(onehot, axis=0) - onehot
        slot_index = lax.optimization_barrier(jnp.sum(before * onehot, axis=1)).astype(jnp.int32)
        destination = (ids_here * MOST + slot_index).astype(jnp.int32)
        buffer = jnp.zeros((CLUSTERS * MOST, K), projected.dtype).at[destination].set(projected)
        return buffer.reshape(CLUSTERS, MOST, K)
    placed = lax.map(place, (device_rows, device_ids, device_noise))
    placed = placed.reshape(N_DP, N_OWNER, CLUSTERS, MOST, K)
    return jnp.transpose(placed, (0, 2, 1, 3, 4))
```

```python
import math

import jax
import jax.numpy as jnp
from jax import lax
from jax.sharding import PartitionSpec as P

CL_DEV = 8
AXES = ("dp", "owner")


def gather_sum(part):
    count = lax.axis_size("dp") * lax.axis_size("owner")
    copies = jnp.broadcast_to(part[None], (count,) + part.shape)
    return jnp.sum(
        lax.all_to_all(copies, AXES, split_axis=0, concat_axis=0, tiled=True), axis=0
    )


def swap_pairs(block):
    return lax.ppermute(block, "dp", [(i, i ^ 1) for i in range(lax.axis_size("dp"))])


def sum_rows(part, wire):
    dp_size, owners = lax.axis_size("dp"), lax.axis_size("owner")
    groups = [
        [d * owners + o for d in range(side, dp_size, 2) for o in range(owners)]
        for side in range(2)
    ]
    members = len(groups[0])
    rows, columns = part.shape
    half = rows // 2
    side = lax.axis_index("dp") % 2
    keep = lax.dynamic_slice_in_dim(part, side * half, half)
    send = lax.dynamic_slice_in_dim(part, (1 - side) * half, half)
    part = (keep + swap_pairs(send)).astype(wire).reshape(members, half // members, columns)
    pieces = lax.all_to_all(
        part, AXES, split_axis=0, concat_axis=0, tiled=True, axis_index_groups=groups
    )
    piece = jnp.sum(pieces.astype(jnp.float32), axis=0)
    copies = jnp.broadcast_to(piece[None], (members,) + piece.shape)
    mine = lax.all_to_all(
        copies, AXES, split_axis=0, concat_axis=0, tiled=True, axis_index_groups=groups
    ).reshape(half, columns)
    other = swap_pairs(mine)
    return jnp.where(
        side == 0, jnp.concatenate([mine, other]), jnp.concatenate([other, mine])
    )


def shards(embeddings, cluster_ids, noise, start_basis):
    highest, high = lax.Precision.HIGHEST, lax.Precision.HIGH
    rows_dev, feature_width = embeddings.shape
    rank_count = start_basis.shape[1]
    owners = lax.axis_size("owner")
    row_total = rows_dev * lax.axis_size("dp") * owners
    column_sum = jnp.sum(embeddings, axis=0, dtype=jnp.float32)
    mean_vec = (
        gather_sum(column_sum.reshape(feature_width // 128, 128)) / row_total
    ).reshape(feature_width)
    second = lax.dot_general(
        embeddings, embeddings, (((0,), (0,)), ((), ())), preferred_element_type=jnp.float32
    )
    mean_here = column_sum / rows_dev
    off_here = mean_here - mean_vec
    share = rows_dev / row_total
    covariance = (
        second / rows_dev - jnp.outer(mean_here, mean_here) + jnp.outer(off_here, off_here)
    ) * share
    image_rows = sum_rows(jnp.dot(covariance, start_basis, precision=high), jnp.bfloat16)
    gram_matrix = jnp.dot(image_rows.T, image_rows, precision=highest)
    lower_factor = jnp.linalg.cholesky(gram_matrix)
    basis_full = lax.linalg.triangular_solve(
        lower_factor, image_rows, left_side=False, lower=True, transpose_a=True
    )
    curved = jnp.dot(covariance, basis_full, precision=high)
    eigen_vals = gather_sum(jnp.sum(basis_full * curved, axis=0)[None])[0]
    signed = math.sqrt(feature_width) * jnp.sum(basis_full, axis=0)
    flip_sign = signed / jnp.maximum(jnp.abs(signed), 1.0)
    whiten = (basis_full * (flip_sign / jnp.sqrt(eigen_vals + 1e-06))).astype(jnp.bfloat16)
    offset = jnp.dot(mean_vec, whiten.astype(jnp.float32), precision=highest)
    clusters = CL_DEV * owners
    capacity = 2 * rows_dev // clusters
    ids_here = cluster_ids[:, 0]
    onehot = (cluster_ids == jnp.arange(clusters, dtype=jnp.int32)[None, :]).astype(jnp.int32)
    before = jnp.cumsum(onehot, axis=0) - onehot
    slot_index = jnp.sum(before * onehot, axis=1)
    destination = ids_here * capacity + slot_index
    projected = (
        jnp.dot(embeddings, whiten, preferred_element_type=jnp.float32)
        - offset
        + noise.astype(jnp.float32)
    ).astype(jnp.bfloat16)
    packed = (
        jnp.zeros((clusters * capacity, rank_count), jnp.bfloat16).at[destination].set(projected)
    )
    packed = packed.reshape(owners, CL_DEV, capacity, rank_count)
    me = lax.axis_index("owner")
    arrived = jnp.zeros((CL_DEV, owners, capacity, rank_count), jnp.bfloat16)
    for step in range(owners):
        block = lax.dynamic_index_in_dim(packed, (me + step) % owners, 0, keepdims=False)
        if step:
            block = lax.ppermute(
                block, "owner", [(i, (i + step) % owners) for i in range(owners)]
            )
        arrived = lax.dynamic_update_index_in_dim(
            arrived, block, (me - step) % owners, 1
        )
    return arrived[None]


def solution(mesh):
    return jax.shard_map(
        shards,
        mesh=mesh,
        in_specs=(
            P(AXES, None),
            P(AXES, None),
            P(AXES, None),
            P(),
        ),
        out_specs=P("dp", "owner", None, None, None),
        check_vma=False,
    )
```

```python
import functools, math
import jax, jax.numpy as jnp
from jax import lax
from jax.experimental import pallas as pl
from jax.experimental.pallas import tpu as pltpu
from jax.sharding import PartitionSpec as P
f32, bf16 = jnp.float32, jnp.bfloat16
HIGHEST = lax.Precision.HIGHEST
CL_DEV = 8

def dot(a, b, dims, precision=None):
    return lax.dot_general(a, b, (dims, ((), ())), precision=precision, preferred_element_type=f32)

def slots_kernel(clusters, capacity, ids_ref, out_ref):
    blocks, width = ids_ref.shape
    names = lax.broadcasted_iota(jnp.int32, (clusters, width), 0)
    above = (lax.broadcasted_iota(jnp.int32, (width, width), 0) < lax.broadcasted_iota(jnp.int32, (width, width), 1)).astype(bf16)
    count = jnp.zeros((clusters, 1), f32)
    for block in range(blocks):
        ids = ids_ref[block : block + 1, :]
        hit = (names == ids).astype(f32)
        before = dot(hit.astype(bf16), above, ((1,), (0,))) + count
        slot = jnp.sum(hit * before, axis=0, keepdims=True)
        out_ref[block : block + 1, :] = ids * capacity + slot.astype(jnp.int32)
        count = count + jnp.sum(hit, axis=1, keepdims=True)

def slots(ids, clusters, capacity):
    rows = ids.shape[0]
    return pl.pallas_call(
        functools.partial(slots_kernel, clusters, capacity),
        out_shape=jax.ShapeDtypeStruct((rows // 256, 256), jnp.int32),
        name="slots",
    )(ids.reshape(rows // 256, 256)).reshape(rows)

PANEL = 32

def split(x):
    top = x.astype(bf16)
    return top, (x - top.astype(f32)).astype(bf16)

def basis_kernel(image_ref, cov_ref, basis_ref, stat_ref, aug):
    image = image_ref[...]
    n = image.shape[1]
    aug[:, :n] = dot(image, image, ((0,), (0,)), HIGHEST)
    aug[:, n:] = (lax.broadcasted_iota(jnp.int32, (n, n), 0) == lax.broadcasted_iota(jnp.int32, (n, n), 1)).astype(f32)
    row = lax.broadcasted_iota(jnp.int32, (PANEL, 1), 0)
    eye = (lax.broadcasted_iota(jnp.int32, (PANEL, PANEL), 0) == lax.broadcasted_iota(jnp.int32, (PANEL, PANEL), 1)).astype(f32)
    for first in range(0, n, PANEL):
        last = first + PANEL
        block = jnp.concatenate([aug[first:last, first:last], eye, jnp.zeros((PANEL, 128 - 2 * PANEL), f32)], axis=1)
        scale = jnp.zeros((PANEL, 1), f32)
        for r in range(PANEL):
            column = block[:, r : r + 1]
            pivot = column[r : r + 1, :]
            pivot_row = block[r : r + 1, :]
            scale = jnp.where(row == r, lax.rsqrt(pivot), scale)
            factor = jnp.where(row > r, column / pivot, 0.0)
            block = block - factor * pivot_row
        inverse = block[:, PANEL : 2 * PANEL] * scale
        upper = dot(inverse, aug[first:last, :], ((1,), (0,)), HIGHEST)
        aug[first:last, :] = upper
        if last < n:
            aug[last:, :] = aug[last:, :] - dot(upper[:, last:n], upper, ((0,), (0,)), HIGHEST)
    basis = dot(image, aug[:, n:], ((1,), (1,)), HIGHEST)
    basis_ref[...] = basis
    basis_top, basis_low = split(basis)
    cov_top, cov_low = split(cov_ref[...])
    mm = ((1,), (0,))
    curved = dot(cov_top, basis_top, mm) + dot(cov_top, basis_low, mm) + dot(cov_low, basis_top, mm)
    stat_ref[0:1, :] = jnp.sum(basis * curved, axis=0, keepdims=True)
    signed = math.sqrt(image.shape[0]) * jnp.sum(basis, axis=0, keepdims=True)
    stat_ref[1:2, :] = signed / jnp.maximum(jnp.abs(signed), 1.0)

def basis_of(image, cov):
    rows, n = image.shape
    return pl.pallas_call(
        basis_kernel,
        out_shape=(jax.ShapeDtypeStruct((rows, n), f32), jax.ShapeDtypeStruct((2, n), f32)),
        scratch_shapes=[pltpu.VMEM((n, 2 * n), f32)],
        compiler_params=pltpu.CompilerParams(vmem_limit_bytes=48 << 20),
        name="basis",
    )(image, cov)

ROWS_STEP = 512

def route_kernel(owners, dest_ref, me_ref, emb_ref, noise_ref, basis_ref, scale_ref, mean_ref, *refs):
    outs, (whiten, offset, fresh, slot) = refs[:owners], refs[owners:]
    step = pl.program_id(0)
    n = basis_ref.shape[1]
    parts = n // 128
    @pl.when(step == 0)
    def _():
        whiten[...] = (basis_ref[...] * scale_ref[...]).astype(bf16)
        offset[...] = dot(mean_ref[...], whiten[...].astype(f32), ((1,), (0,)), HIGHEST)
        slot[...] = jnp.zeros_like(slot)
    values = dot(emb_ref[...], whiten[...], ((1,), (0,))) - offset[...] + noise_ref[...].astype(f32)
    for part in range(parts):
        fresh[part] = values[:, part * 128 : (part + 1) * 128]
    first = step * ROWS_STEP
    def move(r, carry):
        d = dest_ref[first + r]
        for part in range(parts):
            slot[part, pl.ds(d, 1), :] = fresh[part, pl.ds(r, 1), :]
        return carry
    lax.fori_loop(0, ROWS_STEP, move, 0, unroll=16)
    @pl.when(step == pl.num_programs(0) - 1)
    def _():
        size = slot.shape[1] // owners
        for k in range(owners):
            at = pl.multiple_of(lax.rem(me_ref[0] + k, owners) * size, size)
            for part in range(parts):
                outs[k][:, part * 128 : (part + 1) * 128] = slot[part, pl.ds(at, size), :].astype(bf16)

def route(dest, me, emb, noise, basis, scale, mean, owners, slot_count):
    rows, width = emb.shape
    n = basis.shape[1]
    size = slot_count // owners
    whole = lambda shape: pl.BlockSpec(shape, lambda i, *_: (0, 0))
    return pl.pallas_call(
        functools.partial(route_kernel, owners),
        grid_spec=pltpu.PrefetchScalarGridSpec(
            num_scalar_prefetch=2, grid=(rows // ROWS_STEP,),
            in_specs=[pl.BlockSpec((ROWS_STEP, width), lambda i, *_: (i, 0)),
                      pl.BlockSpec((ROWS_STEP, n), lambda i, *_: (i, 0)),
                      whole((width, n)), whole((1, n)), whole((1, width))],
            out_specs=[whole((size, n))] * owners,
            scratch_shapes=[pltpu.VMEM((width, n), bf16), pltpu.VMEM((1, n), f32),
                            pltpu.VMEM((n // 128, ROWS_STEP, 128), f32), pltpu.VMEM((n // 128, slot_count, 128), f32)]),
        out_shape=[jax.ShapeDtypeStruct((size, n), bf16)] * owners,
        compiler_params=pltpu.CompilerParams(vmem_limit_bytes=48 << 20, dimension_semantics=("arbitrary",)),
        name="route",
    )(dest, me, emb, noise, basis, scale, mean)

AXES = ("dp", "owner")


def gather_sum(part):
    count = lax.axis_size("dp") * lax.axis_size("owner")
    copies = jnp.broadcast_to(part[None], (count,) + part.shape)
    return jnp.sum(
        lax.all_to_all(copies, AXES, split_axis=0, concat_axis=0, tiled=True), axis=0
    )


def swap_pairs(block):
    return lax.ppermute(block, "dp", [(i, i ^ 1) for i in range(lax.axis_size("dp"))])


def sum_rows(part):
    dp_size, owners = lax.axis_size("dp"), lax.axis_size("owner")
    groups = [
        [d * owners + o for d in range(side, dp_size, 2) for o in range(owners)]
        for side in range(2)
    ]
    members = len(groups[0])
    rows, columns = part.shape
    half = rows // 2
    side = lax.axis_index("dp") % 2
    keep = lax.dynamic_slice_in_dim(part, side * half, half)
    send = lax.dynamic_slice_in_dim(part, (1 - side) * half, half)
    part = (keep + swap_pairs(send)).reshape(members, half // members, columns)
    pieces = lax.all_to_all(
        part, AXES, split_axis=0, concat_axis=0, tiled=True, axis_index_groups=groups
    )
    piece = jnp.sum(pieces, axis=0)
    copies = jnp.broadcast_to(piece[None], (members,) + piece.shape)
    mine = lax.all_to_all(
        copies, AXES, split_axis=0, concat_axis=0, tiled=True, axis_index_groups=groups
    ).reshape(half, columns)
    other = swap_pairs(mine)
    return jnp.where(
        side == 0, jnp.concatenate([mine, other]), jnp.concatenate([other, mine])
    )


def shards(embeddings, cluster_ids, noise, start_basis):
    rows_dev, feature_width = embeddings.shape
    rank_count = start_basis.shape[1]
    owners = lax.axis_size("owner")
    row_total = rows_dev * lax.axis_size("dp") * owners
    clusters = CL_DEV * owners
    capacity = 2 * rows_dev // clusters
    destination = slots(cluster_ids[:, 0], clusters, capacity)
    column_sum = jnp.sum(embeddings, axis=0, dtype=f32)
    mean_vec = (
        gather_sum(column_sum.reshape(feature_width // 128, 128)) / row_total
    ).reshape(feature_width)
    second = lax.dot_general(
        embeddings, embeddings, (((0,), (0,)), ((), ())), preferred_element_type=f32
    )
    mean_here = column_sum / rows_dev
    off_here = mean_here - mean_vec
    covariance = (
        second / rows_dev - jnp.outer(mean_here, mean_here) + jnp.outer(off_here, off_here)
    ) * (rows_dev / row_total)
    image_rows = sum_rows(jnp.dot(covariance, start_basis, precision=lax.Precision.HIGH))
    basis_full, stats = basis_of(image_rows, covariance)
    eigen_vals = gather_sum(stats[0:1])
    scale = stats[1:2] / jnp.sqrt(eigen_vals + 1e-06)
    me = lax.axis_index("owner").astype(jnp.int32)
    blocks = route(
        destination, me[None], embeddings, noise, basis_full, scale, mean_vec[None],
        owners, clusters * capacity,
    )
    arrived = jnp.zeros((CL_DEV, owners, capacity, rank_count), bf16)
    for step in range(owners):
        block = blocks[step]
        if step:
            block = lax.ppermute(
                block, "owner", [(i, (i + step) % owners) for i in range(owners)]
            )
        arrived = lax.dynamic_update_index_in_dim(
            arrived, block.reshape(CL_DEV, capacity, rank_count), (me - step) % owners, 1
        )
    return arrived[None]


def solution(mesh):
    return jax.shard_map(
        shards,
        mesh=mesh,
        in_specs=(P(AXES, None), P(AXES, None), P(AXES, None), P()),
        out_specs=P("dp", "owner", None, None, None),
        check_vma=False,
    )
```

```python
import functools
import math

import jax
import jax.numpy as jnp
from jax import lax
from jax.experimental import pallas as pl
from jax.experimental.pallas import tpu as pltpu
from jax.sharding import PartitionSpec as P

f32, bf16 = jnp.float32, jnp.bfloat16
HIGHEST = lax.Precision.HIGHEST
AXES = ("dp", "owner")
CL_DEV = 8
PANEL = 64
GROUP = 16
ROWS_STEP = 512


def dot(a, b, dims, precision=None):
    return lax.dot_general(a, b, (dims, ((), ())), precision=precision, preferred_element_type=f32)


def split(x):
    top = x.astype(bf16)
    return top, (x - top.astype(f32)).astype(bf16)


def grant(*order):
    return pltpu.CompilerParams(vmem_limit_bytes=48 << 20, dimension_semantics=order or None)


def slots_kernel(clusters, capacity, ids_ref, out_ref):
    blocks, width = ids_ref.shape
    names = lax.broadcasted_iota(jnp.int32, (clusters, width), 0)
    above = (
        lax.broadcasted_iota(jnp.int32, (width, width), 0)
        < lax.broadcasted_iota(jnp.int32, (width, width), 1)
    ).astype(bf16)
    count = jnp.zeros((clusters, 1), f32)
    for block in range(blocks):
        ids = ids_ref[block : block + 1, :]
        hit = (names == ids).astype(f32)
        before = dot(hit.astype(bf16), above, ((1,), (0,))) + count
        slot = jnp.sum(hit * before, axis=0, keepdims=True)
        out_ref[block : block + 1, :] = ids * capacity + slot.astype(jnp.int32)
        count = count + jnp.sum(hit, axis=1, keepdims=True)


def slots(ids, clusters, capacity):
    rows = ids.shape[0]
    return pl.pallas_call(
        functools.partial(slots_kernel, clusters, capacity),
        out_shape=jax.ShapeDtypeStruct((rows // 128, 128), jnp.int32),
        cost_estimate=pl.CostEstimate(flops=1 << 30, bytes_accessed=1 << 22, transcendentals=0),
        name="slots",
    )(ids.reshape(rows // 128, 128)).reshape(rows)


def moments_kernel(devices, emb_ref, start_ref, cov_ref, image_ref, mean_ref, total):
    step = pl.program_id(0)
    width, n = start_ref.shape
    tile = min(256, width)

    @pl.when(step == 0)
    def _():
        total[...] = jnp.zeros_like(total)
        mean_ref[...] = jnp.zeros_like(mean_ref)

    rows = emb_ref[...]
    mean_ref[...] += jnp.sum(rows.astype(f32), axis=0, keepdims=True)
    for at in range(0, width, tile):
        total[at : at + tile, at:] += dot(rows[:, at : at + tile], rows[:, at:], ((0,), (0,)))

    @pl.when(step == pl.num_programs(0) - 1)
    def _():
        share = 1.0 / (rows.shape[0] * pl.num_programs(0))
        mean = mean_ref[...] * share
        mean_ref[...] = mean
        start = start_ref[...]
        start_top, start_low = split(start)
        along = dot(mean, start, ((1,), (0,)), HIGHEST)
        mm = ((1,), (0,))
        down = [
            jnp.transpose(jnp.broadcast_to(mean[:, at : at + 128], (128, 128)))
            for at in range(0, width, 128)
        ]
        for at in range(0, width, 128):
            for to in range(at // tile * tile, width, 128):
                block = total[at : at + 128, to : to + 128] * share
                block = block - down[at // 128] * mean[:, to : to + 128]
                cov_ref[at : at + 128, to : to + 128] = block
                if to // tile != at // tile:
                    cov_ref[to : to + 128, at : at + 128] = jnp.transpose(block)
        piece = width // devices
        for at in range(0, width, 128):
            top, low = split(cov_ref[at : at + 128, :])
            image = dot(top, start_top, mm) + dot(top, start_low, mm) + dot(low, start_top, mm)
            for half in range(n // 128):
                part = image[:, half * 128 : half * 128 + 128]
                part = part + down[at // 128] * along[:, half * 128 : half * 128 + 128]
                for sub in range(128 // piece):
                    image_ref[at // piece + sub, half * piece : half * piece + piece, :] = part[
                        sub * piece : sub * piece + piece
                    ]
        extra = n // 128 * piece
        for row in range(width // 128):
            image_ref[:, extra + row : extra + row + 1, :] = jnp.broadcast_to(
                mean[:, row * 128 : row * 128 + 128][None], (devices, 1, 128)
            )


def moments(emb, start, devices):
    rows, width = emb.shape
    n = start.shape[1]
    piece = width // devices
    step = rows // 8
    tall = n // 128 * piece + width // 128
    whole = lambda *shape: pl.BlockSpec(shape, lambda i: (0,) * len(shape))
    return pl.pallas_call(
        functools.partial(moments_kernel, devices),
        grid=(8,),
        in_specs=[pl.BlockSpec((step, width), lambda i: (i, 0)), whole(width, n)],
        out_specs=[whole(width, width), whole(devices, tall, 128), whole(1, width)],
        out_shape=[
            jax.ShapeDtypeStruct((width, width), f32),
            jax.ShapeDtypeStruct((devices, tall, 128), f32),
            jax.ShapeDtypeStruct((1, width), f32),
        ],
        scratch_shapes=[pltpu.VMEM((width, width), f32)],
        compiler_params=grant("arbitrary"),
        name="moments",
    )(emb, start)


def basis_kernel(
    devices, side_ref, mine_ref, other_ref, mean_ref, here_ref, start_ref, cov_ref,
    basis_ref, flip_ref, eigen_ref, image_at, aug,
):
    width, n = start_ref.shape
    members, piece = mine_ref.shape[0], width // devices
    half = width // 2
    share = 1.0 / devices
    side = side_ref[0]
    for from_ref, at in ((mine_ref, side), (other_ref, 1 - side)):
        first = pl.multiple_of(at * half, half)
        for member in range(members):
            for part in range(n // 128):
                image_at[
                    pl.ds(first + member * piece, piece), part * 128 : part * 128 + 128
                ] = from_ref[member, part * piece : part * piece + piece, :]
    along = jnp.zeros((1, n), f32)
    for row in range(width // 128):
        along += dot(
            mean_ref[row : row + 1, :], start_ref[row * 128 : row * 128 + 128, :], ((1,), (0,)), HIGHEST
        )
    for row in range(width // 128):
        at = slice(row * 128, row * 128 + 128)
        down = jnp.transpose(jnp.broadcast_to(mean_ref[row : row + 1, :], (128, 128)))
        for part in range(0, n, 128):
            image_at[at, part : part + 128] = (
                image_at[at, part : part + 128] * share - down * along[:, part : part + 128]
            )
    image = image_at[...]
    aug[:, :n] = dot(image, image, ((0,), (0,)), HIGHEST)
    aug[:, n:] = (
        lax.broadcasted_iota(jnp.int32, (n, n), 0) == lax.broadcasted_iota(jnp.int32, (n, n), 1)
    ).astype(f32)
    row = lax.broadcasted_iota(jnp.int32, (PANEL, 2 * PANEL), 0)
    eye = (
        lax.broadcasted_iota(jnp.int32, (PANEL, PANEL), 0)
        == lax.broadcasted_iota(jnp.int32, (PANEL, PANEL), 1)
    ).astype(f32)
    for first in range(0, n, PANEL):
        last = first + PANEL
        block = jnp.concatenate([aug[first:last, first:last], eye], axis=1)
        scale = jnp.zeros((PANEL, 2 * PANEL), f32)
        for lead in range(0, PANEL, GROUP):
            columns = [
                jnp.broadcast_to(block[:, lead + i : lead + i + 1], (PANEL, 2 * PANEL))
                for i in range(GROUP)
            ]
            pivots = [block[lead + i : lead + i + 1, :] for i in range(GROUP)]
            for i in range(GROUP):
                at = lead + i
                pivot = columns[i][at : at + 1, :]
                scale = jnp.where(row == at, lax.rsqrt(pivot), scale)
                factor = jnp.where(row > at, columns[i] * (1.0 / pivot), 0.0)
                for j in range(i + 1, GROUP):
                    columns[j] = columns[j] - factor * columns[j][at : at + 1, :]
                for j in range(i + 1, GROUP):
                    pivots[j] = pivots[j] - factor[lead + j : lead + j + 1, :] * pivots[i]
                block = block - factor * pivots[i]
        inverse = block[:, PANEL:] * scale[:, :PANEL]
        upper = dot(inverse, aug[first:last, :], ((1,), (0,)), HIGHEST)
        aug[first:last, :] = upper
        if last < n:
            aug[last:, :] = aug[last:, :] - dot(
                upper[:, last:n], upper, ((0,), (0,)), HIGHEST
            )
    basis = dot(image, aug[:, n:], ((1,), (1,)), HIGHEST)
    basis_ref[...] = basis
    basis_top, basis_low = split(basis)
    cov_top, cov_low = split(cov_ref[...])
    mm = ((1,), (0,))
    curved = dot(cov_top, basis_top, mm) + dot(cov_top, basis_low, mm) + dot(cov_low, basis_top, mm)
    eigen = jnp.sum(basis * curved, axis=0, keepdims=True)
    apart = jnp.zeros((1, n), f32)
    for row in range(width // 128):
        off_here = here_ref[:, row * 128 : row * 128 + 128] - mean_ref[row : row + 1, :]
        apart += dot(off_here, basis_ref[row * 128 : row * 128 + 128, :], ((1,), (0,)), HIGHEST)
    eigen = (eigen + apart * apart) * share
    eigen_ref[...] = jnp.broadcast_to(eigen[None], eigen_ref.shape)
    signed = math.sqrt(width) * jnp.sum(basis, axis=0, keepdims=True)
    flip_ref[...] = signed / jnp.maximum(jnp.abs(signed), 1.0)


def basis_of(side, mine, other, mean, here, start, cov, devices):
    width, n = start.shape
    vmem = pl.BlockSpec(memory_space=pltpu.VMEM)
    return pl.pallas_call(
        functools.partial(basis_kernel, devices),
        in_specs=[pl.BlockSpec(memory_space=pltpu.SMEM)] + [vmem] * 6,
        out_shape=(
            jax.ShapeDtypeStruct((width, n), f32),
            jax.ShapeDtypeStruct((1, n), f32),
            jax.ShapeDtypeStruct((devices, 1, n), f32),
        ),
        scratch_shapes=[pltpu.VMEM((width, n), f32), pltpu.VMEM((n, 2 * n), f32)],
        compiler_params=grant(),
        name="basis",
    )(side, mine, other, mean, here, start, cov)


def route_kernel(
    owners, dest_ref, me_ref, emb_ref, noise_ref, basis_ref, flip_ref, eigen_ref, mean_ref, *refs
):
    outs, (whiten, offset, fresh, slot) = refs[:owners], refs[owners:]
    step = pl.program_id(0)
    n = basis_ref.shape[1]
    parts = n // 128

    @pl.when(step == 0)
    def _():
        eigen = jnp.sum(eigen_ref[...], axis=0)
        whiten[...] = (basis_ref[...] * (flip_ref[...] / jnp.sqrt(eigen + 1e-06))).astype(bf16)
        shift = jnp.zeros((1, n), f32)
        for row in range(mean_ref.shape[0]):
            at = slice(row * 128, row * 128 + 128)
            shift += dot(mean_ref[row : row + 1, :], whiten[at, :].astype(f32), ((1,), (0,)), HIGHEST)
        offset[...] = shift
        slot[...] = jnp.zeros_like(slot)

    values = dot(emb_ref[...], whiten[...], ((1,), (0,))) - offset[...] + noise_ref[...].astype(f32)
    for part in range(parts):
        fresh[part] = values[:, part * 128 : (part + 1) * 128]
    first = step * ROWS_STEP

    def move(r, carry):
        at = dest_ref[first + r]
        for part in range(parts):
            slot[part, pl.ds(at, 1), :] = fresh[part, pl.ds(r, 1), :]
        return carry

    lax.fori_loop(0, ROWS_STEP, move, 0, unroll=16)

    @pl.when(step == pl.num_programs(0) - 1)
    def _():
        size = slot.shape[1] // owners
        for k in range(owners):
            at = pl.multiple_of(lax.rem(me_ref[0] + k, owners) * size, size)
            for part in range(parts):
                outs[k][:, part * 128 : (part + 1) * 128] = slot[part, pl.ds(at, size), :].astype(bf16)


def route(dest, me, emb, noise, basis, flip, eigen, mean, owners, slot_count):
    rows, width = emb.shape
    n = basis.shape[1]
    size = slot_count // owners
    whole = lambda array: pl.BlockSpec(array.shape, lambda i, *_: (0,) * array.ndim)
    return pl.pallas_call(
        functools.partial(route_kernel, owners),
        grid_spec=pltpu.PrefetchScalarGridSpec(
            num_scalar_prefetch=2,
            grid=(rows // ROWS_STEP,),
            in_specs=[
                pl.BlockSpec((ROWS_STEP, width), lambda i, *_: (i, 0)),
                pl.BlockSpec((ROWS_STEP, n), lambda i, *_: (i, 0)),
                whole(basis), whole(flip), whole(eigen), whole(mean),
            ],
            out_specs=[pl.BlockSpec((size, n), lambda i, *_: (0, 0))] * owners,
            scratch_shapes=[
                pltpu.VMEM((width, n), bf16),
                pltpu.VMEM((1, n), f32),
                pltpu.VMEM((n // 128, ROWS_STEP, 128), f32),
                pltpu.VMEM((n // 128, slot_count, 128), f32),
            ],
        ),
        out_shape=[jax.ShapeDtypeStruct((size, n), bf16)] * owners,
        compiler_params=grant("arbitrary"),
        name="route",
    )(dest, me, emb, noise, basis, flip, eigen, mean)


def swap_pairs(block):
    return lax.ppermute(block, "dp", [(i, i ^ 1) for i in range(lax.axis_size("dp"))])


def exchange(blocks, groups=None):
    return lax.all_to_all(
        blocks, AXES, split_axis=0, concat_axis=0, tiled=True, axis_index_groups=groups
    )


def shards(embeddings, cluster_ids, noise, start_basis):
    rows_dev, width = embeddings.shape
    n = start_basis.shape[1]
    dp_size, owners = lax.axis_size("dp"), lax.axis_size("owner")
    devices = dp_size * owners
    clusters = CL_DEV * owners
    capacity = 2 * rows_dev // clusters
    destination = slots(cluster_ids[:, 0], clusters, capacity)
    covariance, parts, mean_here = moments(embeddings, start_basis, devices)

    groups = [
        [d * owners + o for d in range(side, dp_size, 2) for o in range(owners)]
        for side in range(2)
    ]
    members = devices // 2
    side = lax.axis_index("dp") % 2
    keep = lax.dynamic_slice_in_dim(parts, side * members, members)
    send = lax.dynamic_slice_in_dim(parts, (1 - side) * members, members)
    piece = jnp.sum(exchange(keep + swap_pairs(send), groups), axis=0)
    tall = piece.shape[0] - width // 128
    mean = piece[tall:] / devices
    mine = exchange(jnp.broadcast_to(piece[None, :tall], (members, tall, 128)), groups)
    other = swap_pairs(mine)

    basis, flip, eigen = basis_of(
        side[None].astype(jnp.int32), mine, other, mean, mean_here, start_basis, covariance, devices
    )
    me = lax.axis_index("owner").astype(jnp.int32)
    blocks = route(
        destination, me[None], embeddings, noise, basis, flip, exchange(eigen), mean,
        owners, clusters * capacity,
    )
    arrived = jnp.zeros((CL_DEV, owners, capacity, n), bf16)
    for step in range(owners):
        block = blocks[step]
        if step:
            block = lax.ppermute(
                block, "owner", [(i, (i + step) % owners) for i in range(owners)]
            )
        arrived = lax.dynamic_update_index_in_dim(
            arrived, block.reshape(CL_DEV, capacity, n), (me - step) % owners, 1
        )
    return arrived[None]


def solution(mesh):
    return jax.shard_map(
        shards,
        mesh=mesh,
        in_specs=(P(AXES, None), P(AXES, None), P(AXES, None), P()),
        out_specs=P("dp", "owner", None, None, None),
        check_vma=False,
    )
```

```python
import functools
import math

import jax
import jax.numpy as jnp
from jax import lax
from jax.experimental import pallas as pl
from jax.experimental.pallas import tpu as pltpu
from jax.sharding import PartitionSpec as P

f32, bf16 = jnp.float32, jnp.bfloat16
HIGHEST = lax.Precision.HIGHEST
AXES = ("dp", "owner")
CL_DEV = 8
PANEL = 64
GROUP = 16
ROWS_STEP = 512
TILE = 16
LEVELS = (24, 25, 26, 28, 32)


def dot(a, b, dims, precision=None):
    return lax.dot_general(a, b, (dims, ((), ())), precision=precision, preferred_element_type=f32)


def split(x):
    top = x.astype(bf16)
    return top, (x - top.astype(f32)).astype(bf16)


def grant(*order):
    return pltpu.CompilerParams(vmem_limit_bytes=48 << 20, dimension_semantics=order or None)


def slots_kernel(capacity, ids_ref, out_ref, count_ref):
    blocks, width = ids_ref.shape
    clusters = count_ref.shape[1]
    names = lax.broadcasted_iota(jnp.int32, (clusters, width), 0)
    above = (
        lax.broadcasted_iota(jnp.int32, (width, width), 0)
        < lax.broadcasted_iota(jnp.int32, (width, width), 1)
    ).astype(bf16)
    count = jnp.zeros((clusters, 1), f32)
    count_ref[...] = jnp.zeros_like(count_ref)
    for block in range(blocks):
        hit = (names == ids_ref[block : block + 1, :]).astype(f32)
        before = dot(hit.astype(bf16), above, ((1,), (0,))) + count
        out_ref[block : block + 1, :] = jnp.sum(hit * before, axis=0, keepdims=True).astype(jnp.int32)
        count_ref[...] += dot(jnp.ones((8, width), bf16), hit.astype(bf16), ((1,), (1,)))
        count = count + jnp.sum(hit, axis=1, keepdims=True)
    tiles = jnp.broadcast_to(((count.astype(jnp.int32) + (TILE - 1)) // TILE).astype(f32), (clusters, width))
    later = lax.broadcasted_iota(jnp.int32, (clusters, clusters), 0)
    early = lax.broadcasted_iota(jnp.int32, (clusters, clusters), 1)
    ahead = (early < later) & (early // CL_DEV == later // CL_DEV)
    start = dot(ahead.astype(bf16), tiles.astype(bf16), ((1,), (0,))) * TILE
    start = start + (names // CL_DEV * (CL_DEV * capacity)).astype(f32)
    for block in range(blocks):
        hit = names == ids_ref[block : block + 1, :]
        first = jnp.sum(jnp.where(hit, start, 0.0), axis=0, keepdims=True)
        out_ref[block : block + 1, :] += first.astype(jnp.int32)


def slots(ids, clusters, capacity):
    rows = ids.shape[0]
    place, count = pl.pallas_call(
        functools.partial(slots_kernel, capacity),
        out_shape=(
            jax.ShapeDtypeStruct((rows // 128, 128), jnp.int32),
            jax.ShapeDtypeStruct((8, clusters), f32),
        ),
        cost_estimate=pl.CostEstimate(flops=1 << 30, bytes_accessed=1 << 22, transcendentals=0),
        name="slots",
    )(ids.reshape(rows // 128, 128))
    return place.reshape(rows), count


def moments_kernel(devices, emb_ref, start_ref, cov_ref, image_ref, mean_ref, total):
    step = pl.program_id(0)
    width, n = start_ref.shape
    tile = min(256, width)

    @pl.when(step == 0)
    def _():
        total[...] = jnp.zeros_like(total)
        mean_ref[...] = jnp.zeros_like(mean_ref)

    rows = emb_ref[...]
    mean_ref[...] += jnp.sum(rows.astype(f32), axis=0, keepdims=True)
    for at in range(0, width, tile):
        total[at : at + tile, at:] += dot(rows[:, at : at + tile], rows[:, at:], ((0,), (0,)))

    @pl.when(step == pl.num_programs(0) - 1)
    def _():
        share = 1.0 / (rows.shape[0] * pl.num_programs(0))
        mean = mean_ref[...] * share
        mean_ref[...] = mean
        start = start_ref[...]
        start_top, start_low = split(start)
        along = dot(mean, start, ((1,), (0,)), HIGHEST)
        mm = ((1,), (0,))
        down = [
            jnp.transpose(jnp.broadcast_to(mean[:, at : at + 128], (128, 128)))
            for at in range(0, width, 128)
        ]
        for at in range(0, width, 128):
            for to in range(at // tile * tile, width, 128):
                block = total[at : at + 128, to : to + 128] * share
                block = block - down[at // 128] * mean[:, to : to + 128]
                cov_ref[at : at + 128, to : to + 128] = block
                if to // tile != at // tile:
                    cov_ref[to : to + 128, at : at + 128] = jnp.transpose(block)
        piece = width // devices
        for at in range(0, width, 128):
            top, low = split(cov_ref[at : at + 128, :])
            image = dot(top, start_top, mm) + dot(top, start_low, mm) + dot(low, start_top, mm)
            for half in range(n // 128):
                part = image[:, half * 128 : half * 128 + 128]
                part = part + down[at // 128] * along[:, half * 128 : half * 128 + 128]
                for sub in range(128 // piece):
                    image_ref[at // piece + sub, half * piece : half * piece + piece, :] = part[
                        sub * piece : sub * piece + piece
                    ]
        extra = n // 128 * piece
        for row in range(width // 128):
            image_ref[:, extra + row : extra + row + 1, :] = jnp.broadcast_to(
                mean[:, row * 128 : row * 128 + 128][None], (devices, 1, 128)
            )


def moments(emb, start, devices):
    rows, width = emb.shape
    n = start.shape[1]
    piece = width // devices
    step = rows // 8
    tall = n // 128 * piece + width // 128
    whole = lambda *shape: pl.BlockSpec(shape, lambda i: (0,) * len(shape))
    return pl.pallas_call(
        functools.partial(moments_kernel, devices),
        grid=(8,),
        in_specs=[pl.BlockSpec((step, width), lambda i: (i, 0)), whole(width, n)],
        out_specs=[whole(width, width), whole(devices, tall, 128), whole(1, width)],
        out_shape=[
            jax.ShapeDtypeStruct((width, width), f32),
            jax.ShapeDtypeStruct((devices, tall, 128), f32),
            jax.ShapeDtypeStruct((1, width), f32),
        ],
        scratch_shapes=[pltpu.VMEM((width, width), f32)],
        compiler_params=grant("arbitrary"),
        name="moments",
    )(emb, start)


def basis_kernel(
    devices, side_ref, mine_ref, other_ref, mean_ref, here_ref, start_ref, cov_ref,
    basis_ref, flip_ref, eigen_ref, image_at, aug,
):
    width, n = start_ref.shape
    members, piece = mine_ref.shape[0], width // devices
    half = width // 2
    share = 1.0 / devices
    side = side_ref[0]
    for from_ref, at in ((mine_ref, side), (other_ref, 1 - side)):
        first = pl.multiple_of(at * half, half)
        for member in range(members):
            for part in range(n // 128):
                image_at[
                    pl.ds(first + member * piece, piece), part * 128 : part * 128 + 128
                ] = from_ref[member, part * piece : part * piece + piece, :]
    along = jnp.zeros((1, n), f32)
    for row in range(width // 128):
        along += dot(
            mean_ref[row : row + 1, :], start_ref[row * 128 : row * 128 + 128, :], ((1,), (0,)), HIGHEST
        )
    for row in range(width // 128):
        at = slice(row * 128, row * 128 + 128)
        down = jnp.transpose(jnp.broadcast_to(mean_ref[row : row + 1, :], (128, 128)))
        for part in range(0, n, 128):
            image_at[at, part : part + 128] = (
                image_at[at, part : part + 128] * share - down * along[:, part : part + 128]
            )
    image = image_at[...]
    aug[:, :n] = dot(image, image, ((0,), (0,)), HIGHEST)
    aug[:, n:] = (
        lax.broadcasted_iota(jnp.int32, (n, n), 0) == lax.broadcasted_iota(jnp.int32, (n, n), 1)
    ).astype(f32)
    row = lax.broadcasted_iota(jnp.int32, (PANEL, 2 * PANEL), 0)
    eye = (
        lax.broadcasted_iota(jnp.int32, (PANEL, PANEL), 0)
        == lax.broadcasted_iota(jnp.int32, (PANEL, PANEL), 1)
    ).astype(f32)
    for first in range(0, n, PANEL):
        last = first + PANEL
        block = jnp.concatenate([aug[first:last, first:last], eye], axis=1)
        scale = jnp.zeros((PANEL, 2 * PANEL), f32)
        for lead in range(0, PANEL, GROUP):
            columns = [
                jnp.broadcast_to(block[:, lead + i : lead + i + 1], (PANEL, 2 * PANEL))
                for i in range(GROUP)
            ]
            pivots = [block[lead + i : lead + i + 1, :] for i in range(GROUP)]
            for i in range(GROUP):
                at = lead + i
                pivot = columns[i][at : at + 1, :]
                scale = jnp.where(row == at, lax.rsqrt(pivot), scale)
                factor = jnp.where(row > at, columns[i] * (1.0 / pivot), 0.0)
                for j in range(i + 1, GROUP):
                    columns[j] = columns[j] - factor * columns[j][at : at + 1, :]
                for j in range(i + 1, GROUP):
                    pivots[j] = pivots[j] - factor[lead + j : lead + j + 1, :] * pivots[i]
                block = block - factor * pivots[i]
        inverse = block[:, PANEL:] * scale[:, :PANEL]
        upper = dot(inverse, aug[first:last, :], ((1,), (0,)), HIGHEST)
        aug[first:last, :] = upper
        if last < n:
            aug[last:, :] = aug[last:, :] - dot(
                upper[:, last:n], upper, ((0,), (0,)), HIGHEST
            )
    basis = dot(image, aug[:, n:], ((1,), (1,)), HIGHEST)
    basis_ref[...] = basis
    basis_top, basis_low = split(basis)
    cov_top, cov_low = split(cov_ref[...])
    mm = ((1,), (0,))
    curved = dot(cov_top, basis_top, mm) + dot(cov_top, basis_low, mm) + dot(cov_low, basis_top, mm)
    eigen = jnp.sum(basis * curved, axis=0, keepdims=True)
    apart = jnp.zeros((1, n), f32)
    for row in range(width // 128):
        off_here = here_ref[:, row * 128 : row * 128 + 128] - mean_ref[row : row + 1, :]
        apart += dot(off_here, basis_ref[row * 128 : row * 128 + 128, :], ((1,), (0,)), HIGHEST)
    eigen = (eigen + apart * apart) * share
    eigen_ref[...] = jnp.broadcast_to(eigen[None], eigen_ref.shape)
    signed = math.sqrt(width) * jnp.sum(basis, axis=0, keepdims=True)
    flip_ref[...] = signed / jnp.maximum(jnp.abs(signed), 1.0)


def basis_of(side, mine, other, mean, here, start, cov, devices):
    width, n = start.shape
    vmem = pl.BlockSpec(memory_space=pltpu.VMEM)
    return pl.pallas_call(
        functools.partial(basis_kernel, devices),
        in_specs=[pl.BlockSpec(memory_space=pltpu.SMEM)] + [vmem] * 6,
        out_shape=(
            jax.ShapeDtypeStruct((width, n), f32),
            jax.ShapeDtypeStruct((1, n), f32),
            jax.ShapeDtypeStruct((devices, 1, n), f32),
        ),
        scratch_shapes=[pltpu.VMEM((width, n), f32), pltpu.VMEM((n, 2 * n), f32)],
        compiler_params=grant(),
        name="basis",
    )(side, mine, other, mean, here, start, cov)


def route_kernel(
    owners, dest_ref, me_ref, emb_ref, noise_ref, basis_ref, flip_ref, eigen_ref, mean_ref, *refs
):
    outs, (whiten, offset, fresh, slot) = refs[:owners], refs[owners:]
    step = pl.program_id(0)
    n = basis_ref.shape[1]
    parts = n // 128

    @pl.when(step == 0)
    def _():
        eigen = jnp.sum(eigen_ref[...], axis=0)
        whiten[...] = (basis_ref[...] * (flip_ref[...] / jnp.sqrt(eigen + 1e-06))).astype(bf16)
        shift = jnp.zeros((1, n), f32)
        for row in range(mean_ref.shape[0]):
            at = slice(row * 128, row * 128 + 128)
            shift += dot(mean_ref[row : row + 1, :], whiten[at, :].astype(f32), ((1,), (0,)), HIGHEST)
        offset[...] = shift

    values = dot(emb_ref[...], whiten[...], ((1,), (0,))) - offset[...] + noise_ref[...].astype(f32)
    for part in range(parts):
        fresh[part] = values[:, part * 128 : (part + 1) * 128]
    first = step * ROWS_STEP

    def move(r, carry):
        at = dest_ref[first + r]
        for part in range(parts):
            slot[part, pl.ds(at, 1), :] = fresh[part, pl.ds(r, 1), :]
        return carry

    lax.fori_loop(0, ROWS_STEP, move, 0, unroll=16)

    @pl.when(step == pl.num_programs(0) - 1)
    def _():
        size, room = slot.shape[1] // owners, outs[0].shape[0]
        for k in range(owners):
            at = pl.multiple_of(lax.rem(me_ref[0] + k, owners) * size, size)
            for part in range(parts):
                outs[k][:, part * 128 : (part + 1) * 128] = slot[part, pl.ds(at, room), :].astype(bf16)


def route(dest, me, emb, noise, basis, flip, eigen, mean, owners, slot_count, room):
    rows, width = emb.shape
    n = basis.shape[1]
    whole = lambda array: pl.BlockSpec(array.shape, lambda i, *_: (0,) * array.ndim)
    return pl.pallas_call(
        functools.partial(route_kernel, owners),
        grid_spec=pltpu.PrefetchScalarGridSpec(
            num_scalar_prefetch=2,
            grid=(rows // ROWS_STEP,),
            in_specs=[
                pl.BlockSpec((ROWS_STEP, width), lambda i, *_: (i, 0)),
                pl.BlockSpec((ROWS_STEP, n), lambda i, *_: (i, 0)),
                whole(basis), whole(flip), whole(eigen), whole(mean),
            ],
            out_specs=[pl.BlockSpec((room, n), lambda i, *_: (0, 0))] * owners,
            scratch_shapes=[
                pltpu.VMEM((width, n), bf16),
                pltpu.VMEM((1, n), f32),
                pltpu.VMEM((n // 128, ROWS_STEP, 128), f32),
                pltpu.VMEM((n // 128, slot_count, 128), f32),
            ],
        ),
        out_shape=[jax.ShapeDtypeStruct((room, n), bf16)] * owners,
        compiler_params=grant("arbitrary"),
        name="route",
    )(dest, me, emb, noise, basis, flip, eigen, mean)


PART = 4


def unpack_kernel(capacity, source_ref, count_ref, block_ref, *refs):
    out_ref = refs[-1]
    lead = pl.program_id(0) * PART
    room, n = block_ref.shape
    base = source_ref[0] * CL_DEV
    tile = lax.fori_loop(
        0, lead, lambda c, at: at + (count_ref[base + c] + (TILE - 1)) // TILE, jnp.int32(0)
    )
    row = lax.broadcasted_iota(jnp.int32, (TILE, n), 0)
    for c in range(PART):
        count = count_ref[base + lead + c]
        for t in range(capacity // TILE):
            at = pl.multiple_of(jnp.minimum(tile + t, room // TILE - 1) * TILE, TILE)
            rows = block_ref[pl.ds(at, TILE), :]
            out_ref[c, 0, t * TILE : t * TILE + TILE, :] = jnp.where(
                row < count - t * TILE, rows, jnp.zeros_like(rows)
            )
        tile = tile + (count + (TILE - 1)) // TILE


def unpack(source, counts, block, arrived, owners, capacity):
    room, n = block.shape
    spec = pl.BlockSpec((PART, 1, capacity, n), lambda i, source_ref, *_: (i, source_ref[0], 0, 0))
    extra = [] if arrived is None else [arrived]
    return pl.pallas_call(
        functools.partial(unpack_kernel, capacity),
        grid_spec=pltpu.PrefetchScalarGridSpec(
            num_scalar_prefetch=2,
            grid=(CL_DEV // PART,),
            in_specs=[pl.BlockSpec((room, n), lambda i, *_: (0, 0))]
            + [pl.BlockSpec(memory_space=pl.ANY)] * len(extra),
            out_specs=spec,
        ),
        out_shape=jax.ShapeDtypeStruct((CL_DEV, owners, capacity, n), bf16),
        input_output_aliases={3: 0} if extra else {},
        compiler_params=grant("arbitrary"),
        cost_estimate=pl.CostEstimate(flops=1 << 20, bytes_accessed=1 << 20, transcendentals=0),
        name="unpack",
    )(source, counts, block, *extra)


def swap_pairs(block):
    return lax.ppermute(block, "dp", [(i, i ^ 1) for i in range(lax.axis_size("dp"))])


def exchange(blocks, groups=None):
    return lax.all_to_all(
        blocks, AXES, split_axis=0, concat_axis=0, tiled=True, axis_index_groups=groups
    )


def shards(embeddings, cluster_ids, noise, start_basis):
    rows_dev, width = embeddings.shape
    n = start_basis.shape[1]
    dp_size, owners = lax.axis_size("dp"), lax.axis_size("owner")
    devices = dp_size * owners
    clusters = CL_DEV * owners
    capacity = 2 * rows_dev // clusters
    place, count = slots(cluster_ids[:, 0], clusters, capacity)
    count = jnp.pad(count, ((0, 0), (0, -clusters % 128)))
    covariance, parts, mean_here = moments(embeddings, start_basis, devices)

    groups = [
        [d * owners + o for d in range(side, dp_size, 2) for o in range(owners)]
        for side in range(2)
    ]
    members = devices // 2
    side = lax.axis_index("dp") % 2
    keep = lax.dynamic_slice_in_dim(parts, side * members, members)
    send = lax.dynamic_slice_in_dim(parts, (1 - side) * members, members)
    piece = jnp.sum(exchange(keep + swap_pairs(send), groups), axis=0)
    tall = piece.shape[0] - width // 128
    mean = piece[tall:] / devices
    sent = jnp.concatenate([piece[:tall], count])
    mine = exchange(jnp.broadcast_to(sent[None], (members,) + sent.shape), groups)
    other = swap_pairs(mine)

    basis, flip, eigen = basis_of(
        side[None].astype(jnp.int32), mine, other, mean, mean_here, start_basis, covariance, devices
    )
    me = lax.axis_index("owner").astype(jnp.int32)
    tables = [t[:, tall, :clusters].astype(jnp.int32) for t in (mine, other)]
    rooms = [level * (CL_DEV * capacity) // 32 for level in LEVELS]
    need = jnp.int32(0)
    for table in tables:
        tiles = (table + (TILE - 1)) // TILE * TILE
        need = jnp.maximum(need, jnp.max(jnp.sum(tiles.reshape(members, owners, CL_DEV), axis=2)))
    level = jnp.sum((need > jnp.array(rooms[:-1], jnp.int32)).astype(jnp.int32))
    row_of = lax.axis_index("dp") // 2 * owners
    counts = lax.dynamic_slice(tables[0], (row_of, me * CL_DEV), (owners, CL_DEV)).reshape(-1)

    def deliver(room, place, me, embeddings, noise, basis, flip, eigen, mean, counts):
        blocks = route(
            place, me[None], embeddings, noise, basis, flip, eigen, mean,
            owners, clusters * capacity, room,
        )
        arrived = None
        for step in range(owners):
            block = blocks[step]
            if step:
                block = lax.ppermute(
                    block, "owner", [(i, (i + step) % owners) for i in range(owners)]
                )
            source = (me - step + owners) % owners
            arrived = unpack(source[None], counts, block, arrived, owners, capacity)
        return arrived

    arrived = lax.switch(
        level,
        [functools.partial(deliver, room) for room in rooms],
        place, me, embeddings, noise, basis, flip, exchange(eigen), mean, counts,
    )
    return arrived[None]


def solution(mesh):
    return jax.shard_map(
        shards,
        mesh=mesh,
        in_specs=(P(AXES, None), P(AXES, None), P(AXES, None), P()),
        out_specs=P("dp", "owner", None, None, None),
        check_vma=False,
    )
```

```python
import functools
import math

import jax
import jax.numpy as jnp
from jax import lax
from jax.experimental import pallas as pl
from jax.experimental.pallas import tpu as pltpu
from jax.sharding import PartitionSpec as P

f32, bf16 = jnp.float32, jnp.bfloat16
HIGHEST = lax.Precision.HIGHEST
AXES = ("dp", "owner")
CL_DEV = 8
PANEL = 64
GROUP = 16
ROWS_STEP = 1024
MOVED = 32
STEPS = 4
TILE = 16
LEVELS = (24, 25, 28, 32)


def dot(a, b, dims, precision=None):
    return lax.dot_general(a, b, (dims, ((), ())), precision=precision, preferred_element_type=f32)


def split(x):
    top = x.astype(bf16)
    return top, (x - top.astype(f32)).astype(bf16)


def grant(*order, room=24):
    return pltpu.CompilerParams(vmem_limit_bytes=room << 20, dimension_semantics=order or None)


def slots_kernel(capacity, ids_ref, out_ref, count_ref):
    blocks, width = ids_ref.shape
    clusters = count_ref.shape[1]
    names = lax.broadcasted_iota(jnp.int32, (clusters, width), 0)
    above = (
        lax.broadcasted_iota(jnp.int32, (width, width), 0)
        < lax.broadcasted_iota(jnp.int32, (width, width), 1)
    ).astype(bf16)
    count = jnp.zeros((clusters, 1), f32)
    count_ref[...] = jnp.zeros_like(count_ref)
    for block in range(blocks):
        hit = (names == ids_ref[block : block + 1, :]).astype(f32)
        before = dot(hit.astype(bf16), above, ((1,), (0,))) + count
        out_ref[block : block + 1, :] = jnp.sum(hit * before, axis=0, keepdims=True).astype(jnp.int32)
        count_ref[...] += dot(jnp.ones((8, width), bf16), hit.astype(bf16), ((1,), (1,)))
        count = count + jnp.sum(hit, axis=1, keepdims=True)
    tiles = jnp.broadcast_to(((count.astype(jnp.int32) + (TILE - 1)) // TILE).astype(f32), (clusters, width))
    later = lax.broadcasted_iota(jnp.int32, (clusters, clusters), 0)
    early = lax.broadcasted_iota(jnp.int32, (clusters, clusters), 1)
    ahead = (early < later) & (early // CL_DEV == later // CL_DEV)
    start = dot(ahead.astype(bf16), tiles.astype(bf16), ((1,), (0,))) * TILE
    start = start + (names // CL_DEV * (CL_DEV * capacity)).astype(f32)
    for block in range(blocks):
        hit = names == ids_ref[block : block + 1, :]
        first = jnp.sum(jnp.where(hit, start, 0.0), axis=0, keepdims=True)
        out_ref[block : block + 1, :] += first.astype(jnp.int32)


def slots(ids, clusters, capacity):
    rows = ids.shape[0]
    place, count = pl.pallas_call(
        functools.partial(slots_kernel, capacity),
        out_shape=(
            jax.ShapeDtypeStruct((rows // 128, 128), jnp.int32),
            jax.ShapeDtypeStruct((8, clusters), f32),
        ),
        cost_estimate=pl.CostEstimate(flops=1 << 30, bytes_accessed=1 << 22, transcendentals=0),
        name="slots",
    )(ids.reshape(rows // 128, 128))
    return place.reshape(rows), count


def moments_kernel(devices, emb_ref, start_ref, cov_ref, image_ref, mean_ref, total):
    step = pl.program_id(0)
    width, n = start_ref.shape
    tile = min(256, width)

    @pl.when(step == 0)
    def _():
        total[...] = jnp.zeros_like(total)
        mean_ref[...] = jnp.zeros_like(mean_ref)

    rows = emb_ref[...]
    mean_ref[...] += jnp.sum(rows.astype(f32), axis=0, keepdims=True)
    for at in range(0, width, tile):
        total[at : at + tile, at:] += dot(rows[:, at : at + tile], rows[:, at:], ((0,), (0,)))

    @pl.when(step == pl.num_programs(0) - 1)
    def _():
        share = 1.0 / (rows.shape[0] * pl.num_programs(0))
        mean = mean_ref[...] * share
        mean_ref[...] = mean
        start = start_ref[...]
        start_top, start_low = split(start)
        along = dot(mean, start, ((1,), (0,)), HIGHEST)
        mm = ((1,), (0,))
        down = [
            jnp.transpose(jnp.broadcast_to(mean[:, at : at + 128], (128, 128)))
            for at in range(0, width, 128)
        ]
        for at in range(0, width, 128):
            for to in range(at // tile * tile, width, 128):
                block = total[at : at + 128, to : to + 128] * share
                block = block - down[at // 128] * mean[:, to : to + 128]
                cov_ref[at : at + 128, to : to + 128] = block
                if to // tile != at // tile:
                    cov_ref[to : to + 128, at : at + 128] = jnp.transpose(block)
        piece = width // devices
        for at in range(0, width, 128):
            top, low = split(cov_ref[at : at + 128, :])
            image = dot(top, start_top, mm) + dot(top, start_low, mm) + dot(low, start_top, mm)
            for half in range(n // 128):
                part = image[:, half * 128 : half * 128 + 128]
                part = part + down[at // 128] * along[:, half * 128 : half * 128 + 128]
                for sub in range(128 // piece):
                    image_ref[at // piece + sub, half * piece : half * piece + piece, :] = part[
                        sub * piece : sub * piece + piece
                    ]
        extra = n // 128 * piece
        for row in range(width // 128):
            image_ref[:, extra + row : extra + row + 1, :] = jnp.broadcast_to(
                mean[:, row * 128 : row * 128 + 128][None], (devices, 1, 128)
            )


def moments(emb, start, devices):
    rows, width = emb.shape
    n = start.shape[1]
    piece = width // devices
    step = rows // STEPS
    tall = n // 128 * piece + width // 128
    whole = lambda *shape: pl.BlockSpec(shape, lambda i: (0,) * len(shape))
    return pl.pallas_call(
        functools.partial(moments_kernel, devices),
        grid=(STEPS,),
        in_specs=[pl.BlockSpec((step, width), lambda i: (i, 0)), whole(width, n)],
        out_specs=[whole(width, width), whole(devices, tall, 128), whole(1, width)],
        out_shape=[
            jax.ShapeDtypeStruct((width, width), f32),
            jax.ShapeDtypeStruct((devices, tall, 128), f32),
            jax.ShapeDtypeStruct((1, width), f32),
        ],
        scratch_shapes=[pltpu.VMEM((width, width), f32)],
        compiler_params=grant("arbitrary"),
        name="moments",
    )(emb, start)


def basis_kernel(
    devices, side_ref, mine_ref, other_ref, mean_ref, here_ref, start_ref, cov_ref,
    basis_ref, flip_ref, eigen_ref, image_at, aug,
):
    width, n = start_ref.shape
    members, piece = mine_ref.shape[0], width // devices
    half = width // 2
    share = 1.0 / devices
    side = side_ref[0]
    for from_ref, at in ((mine_ref, side), (other_ref, 1 - side)):
        first = pl.multiple_of(at * half, half)
        for member in range(members):
            for part in range(n // 128):
                image_at[
                    pl.ds(first + member * piece, piece), part * 128 : part * 128 + 128
                ] = from_ref[member, part * piece : part * piece + piece, :]
    along = jnp.zeros((1, n), f32)
    for row in range(width // 128):
        along += dot(
            mean_ref[row : row + 1, :], start_ref[row * 128 : row * 128 + 128, :], ((1,), (0,)), HIGHEST
        )
    for row in range(width // 128):
        at = slice(row * 128, row * 128 + 128)
        down = jnp.transpose(jnp.broadcast_to(mean_ref[row : row + 1, :], (128, 128)))
        for part in range(0, n, 128):
            image_at[at, part : part + 128] = (
                image_at[at, part : part + 128] * share - down * along[:, part : part + 128]
            )
    image = image_at[...]
    aug[:, :n] = dot(image, image, ((0,), (0,)), HIGHEST)
    aug[:, n:] = (
        lax.broadcasted_iota(jnp.int32, (n, n), 0) == lax.broadcasted_iota(jnp.int32, (n, n), 1)
    ).astype(f32)
    eye = (
        lax.broadcasted_iota(jnp.int32, (PANEL, PANEL), 0)
        == lax.broadcasted_iota(jnp.int32, (PANEL, PANEL), 1)
    ).astype(f32)
    for first in range(0, n, PANEL):
        last = first + PANEL
        active = jnp.concatenate([aug[first:last, first:last], eye], axis=1)
        done = []
        for lead in range(0, PANEL, GROUP):
            row = lax.broadcasted_iota(jnp.int32, active.shape, 0)
            columns = [
                jnp.broadcast_to(active[:, lead + i : lead + i + 1], active.shape)
                for i in range(GROUP)
            ]
            pivots = [active[i : i + 1, :] for i in range(GROUP)]
            scale = jnp.zeros((GROUP, 2 * PANEL), f32)
            for i in range(GROUP):
                pivot = columns[i][i : i + 1, :]
                scale = jnp.where(row[:GROUP] == i, lax.rsqrt(pivot), scale)
                factor = jnp.where(row > i, columns[i] * (1.0 / pivot), 0.0)
                for j in range(i + 1, GROUP):
                    columns[j] = columns[j] - factor * columns[j][i : i + 1, :]
                for j in range(i + 1, GROUP):
                    pivots[j] = pivots[j] - factor[j : j + 1, :] * pivots[i]
                active = active - factor * pivots[i]
            done.append(active[:GROUP] * scale)
            active = active[GROUP:]
        inverse = jnp.concatenate(done, axis=0)[:, PANEL:]
        upper = dot(inverse, aug[first:last, :], ((1,), (0,)), HIGHEST)
        aug[first:last, :] = upper
        if last < n:
            aug[last:, :] = aug[last:, :] - dot(
                upper[:, last:n], upper, ((0,), (0,)), HIGHEST
            )
    basis = dot(image, aug[:, n:], ((1,), (1,)), HIGHEST)
    basis_ref[...] = basis
    basis_top, basis_low = split(basis)
    cov_top, cov_low = split(cov_ref[...])
    mm = ((1,), (0,))
    curved = dot(cov_top, basis_top, mm) + dot(cov_top, basis_low, mm) + dot(cov_low, basis_top, mm)
    eigen = jnp.sum(basis * curved, axis=0, keepdims=True)
    apart = jnp.zeros((1, n), f32)
    for row in range(width // 128):
        off_here = here_ref[:, row * 128 : row * 128 + 128] - mean_ref[row : row + 1, :]
        apart += dot(off_here, basis_ref[row * 128 : row * 128 + 128, :], ((1,), (0,)), HIGHEST)
    eigen = (eigen + apart * apart) * share
    eigen_ref[...] = jnp.broadcast_to(eigen[None], eigen_ref.shape)
    signed = math.sqrt(width) * jnp.sum(basis, axis=0, keepdims=True)
    flip_ref[...] = signed / jnp.maximum(jnp.abs(signed), 1.0)


def basis_of(side, mine, other, mean, here, start, cov, devices):
    width, n = start.shape
    vmem = pl.BlockSpec(memory_space=pltpu.VMEM)
    return pl.pallas_call(
        functools.partial(basis_kernel, devices),
        in_specs=[pl.BlockSpec(memory_space=pltpu.SMEM)] + [vmem] * 6,
        out_shape=(
            jax.ShapeDtypeStruct((width, n), f32),
            jax.ShapeDtypeStruct((1, n), f32),
            jax.ShapeDtypeStruct((devices, 1, n), f32),
        ),
        scratch_shapes=[pltpu.VMEM((width, n), f32), pltpu.VMEM((n, 2 * n), f32)],
        compiler_params=grant(),
        name="basis",
    )(side, mine, other, mean, here, start, cov)


def route_kernel(
    owners, dest_ref, me_ref, emb_ref, noise_ref, basis_ref, flip_ref, eigen_ref, mean_ref, *refs
):
    outs, (whiten, offset, fresh, slot) = refs[:owners], refs[owners:]
    step = pl.program_id(0)
    n = basis_ref.shape[1]
    parts = n // 128

    @pl.when(step == 0)
    def _():
        eigen = jnp.sum(eigen_ref[...], axis=0)
        whiten[...] = (basis_ref[...] * (flip_ref[...] / jnp.sqrt(eigen + 1e-06))).astype(bf16)
        shift = jnp.zeros((1, n), f32)
        for row in range(mean_ref.shape[0]):
            at = slice(row * 128, row * 128 + 128)
            shift += dot(mean_ref[row : row + 1, :], whiten[at, :].astype(f32), ((1,), (0,)), HIGHEST)
        offset[...] = shift

    values = dot(emb_ref[...], whiten[...], ((1,), (0,))) - offset[...] + noise_ref[...].astype(f32)
    for part in range(parts):
        fresh[part] = values[:, part * 128 : (part + 1) * 128]
    first = step * ROWS_STEP

    def move(group, carry):
        lead = group * MOVED
        ats = [dest_ref[first + lead + r] for r in range(MOVED)]
        for part in range(parts):
            rows = [fresh[part, pl.ds(lead + r, 1), :] for r in range(MOVED)]
            for at, row in zip(ats, rows):
                slot[part, pl.ds(at, 1), :] = row
        return carry

    lax.fori_loop(0, ROWS_STEP // MOVED, move, 0)

    @pl.when(step == pl.num_programs(0) - 1)
    def _():
        size, room = slot.shape[1] // owners, outs[0].shape[0]
        for k in range(owners):
            at = pl.multiple_of(lax.rem(me_ref[0] + k, owners) * size, size)
            for part in range(parts):
                outs[k][:, part * 128 : (part + 1) * 128] = slot[part, pl.ds(at, room), :].astype(bf16)


def route(dest, me, emb, noise, basis, flip, eigen, mean, owners, slot_count, room):
    rows, width = emb.shape
    n = basis.shape[1]
    whole = lambda array: pl.BlockSpec(array.shape, lambda i, *_: (0,) * array.ndim)
    return pl.pallas_call(
        functools.partial(route_kernel, owners),
        grid_spec=pltpu.PrefetchScalarGridSpec(
            num_scalar_prefetch=2,
            grid=(rows // ROWS_STEP,),
            in_specs=[
                pl.BlockSpec((ROWS_STEP, width), lambda i, *_: (i, 0)),
                pl.BlockSpec((ROWS_STEP, n), lambda i, *_: (i, 0)),
                whole(basis), whole(flip), whole(eigen), whole(mean),
            ],
            out_specs=[pl.BlockSpec((room, n), lambda i, *_: (0, 0))] * owners,
            scratch_shapes=[
                pltpu.VMEM((width, n), bf16),
                pltpu.VMEM((1, n), f32),
                pltpu.VMEM((n // 128, ROWS_STEP, 128), f32),
                pltpu.VMEM((n // 128, slot_count, 128), f32),
            ],
        ),
        out_shape=[jax.ShapeDtypeStruct((room, n), bf16)] * owners,
        compiler_params=grant("arbitrary"),
        name="route",
    )(dest, me, emb, noise, basis, flip, eigen, mean)


PART = 4


def unpack_kernel(capacity, source_ref, count_ref, block_ref, *refs):
    out_ref = refs[-1]
    lead = pl.program_id(0) * PART
    room, n = block_ref.shape
    base = source_ref[0] * CL_DEV
    tile = lax.fori_loop(
        0, lead, lambda c, at: at + (count_ref[base + c] + (TILE - 1)) // TILE, jnp.int32(0)
    )
    row = lax.broadcasted_iota(jnp.int32, (TILE, n), 0)
    for c in range(PART):
        count = count_ref[base + lead + c]
        for t in range(capacity // TILE):
            at = pl.multiple_of(jnp.minimum(tile + t, room // TILE - 1) * TILE, TILE)
            rows = block_ref[pl.ds(at, TILE), :]
            out_ref[c, 0, t * TILE : t * TILE + TILE, :] = jnp.where(
                row < count - t * TILE, rows, jnp.zeros_like(rows)
            )
        tile = tile + (count + (TILE - 1)) // TILE


def unpack(source, counts, block, arrived, owners, capacity):
    room, n = block.shape
    spec = pl.BlockSpec((PART, 1, capacity, n), lambda i, source_ref, *_: (i, source_ref[0], 0, 0))
    extra = [] if arrived is None else [arrived]
    return pl.pallas_call(
        functools.partial(unpack_kernel, capacity),
        grid_spec=pltpu.PrefetchScalarGridSpec(
            num_scalar_prefetch=2,
            grid=(CL_DEV // PART,),
            in_specs=[pl.BlockSpec((room, n), lambda i, *_: (0, 0))]
            + [pl.BlockSpec(memory_space=pl.ANY)] * len(extra),
            out_specs=spec,
        ),
        out_shape=jax.ShapeDtypeStruct((CL_DEV, owners, capacity, n), bf16),
        input_output_aliases={3: 0} if extra else {},
        compiler_params=grant("arbitrary"),
        cost_estimate=pl.CostEstimate(flops=1 << 20, bytes_accessed=1 << 20, transcendentals=0),
        name="unpack",
    )(source, counts, block, *extra)


def swap_pairs(block):
    return lax.ppermute(block, "dp", [(i, i ^ 1) for i in range(lax.axis_size("dp"))])


def exchange(blocks, groups=None):
    return lax.all_to_all(
        blocks, AXES, split_axis=0, concat_axis=0, tiled=True, axis_index_groups=groups
    )


def shards(embeddings, cluster_ids, noise, start_basis):
    rows_dev, width = embeddings.shape
    n = start_basis.shape[1]
    dp_size, owners = lax.axis_size("dp"), lax.axis_size("owner")
    devices = dp_size * owners
    clusters = CL_DEV * owners
    capacity = 2 * rows_dev // clusters
    place, count = slots(cluster_ids[:, 0], clusters, capacity)
    count = jnp.pad(count, ((0, 0), (0, -clusters % 128)))
    covariance, parts, mean_here = moments(embeddings, start_basis, devices)

    groups = [
        [d * owners + o for d in range(side, dp_size, 2) for o in range(owners)]
        for side in range(2)
    ]
    members = devices // 2
    side = lax.axis_index("dp") % 2
    keep = lax.dynamic_slice_in_dim(parts, side * members, members)
    send = lax.dynamic_slice_in_dim(parts, (1 - side) * members, members)
    piece = jnp.sum(exchange(keep + swap_pairs(send), groups), axis=0)
    tall = piece.shape[0] - width // 128
    mean = piece[tall:] / devices
    sent = jnp.concatenate([piece[:tall], count])
    mine = exchange(jnp.broadcast_to(sent[None], (members,) + sent.shape), groups)
    other = swap_pairs(mine)

    basis, flip, eigen = basis_of(
        side[None].astype(jnp.int32), mine, other, mean, mean_here, start_basis, covariance, devices
    )
    me = lax.axis_index("owner").astype(jnp.int32)
    tables = [t[:, tall, :clusters].astype(jnp.int32) for t in (mine, other)]
    rooms = [level * (CL_DEV * capacity) // 32 for level in LEVELS]
    need = jnp.int32(0)
    for table in tables:
        tiles = (table + (TILE - 1)) // TILE * TILE
        need = jnp.maximum(need, jnp.max(jnp.sum(tiles.reshape(members, owners, CL_DEV), axis=2)))
    level = jnp.sum((need > jnp.array(rooms[:-1], jnp.int32)).astype(jnp.int32))
    row_of = lax.axis_index("dp") // 2 * owners
    counts = lax.dynamic_slice(tables[0], (row_of, me * CL_DEV), (owners, CL_DEV)).reshape(-1)

    def deliver(room, place, me, embeddings, noise, basis, flip, eigen, mean, counts):
        blocks = route(
            place, me[None], embeddings, noise, basis, flip, eigen, mean,
            owners, clusters * capacity, room,
        )
        arrived = None
        for step in range(owners):
            block = blocks[step]
            if step:
                block = lax.ppermute(
                    block, "owner", [(i, (i + step) % owners) for i in range(owners)]
                )
            source = (me - step + owners) % owners
            arrived = unpack(source[None], counts, block, arrived, owners, capacity)
        return arrived

    arrived = lax.switch(
        level,
        [functools.partial(deliver, room) for room in rooms],
        place, me, embeddings, noise, basis, flip, exchange(eigen), mean, counts,
    )
    return arrived[None]


def solution(mesh):
    return jax.shard_map(
        shards,
        mesh=mesh,
        in_specs=(P(AXES, None), P(AXES, None), P(AXES, None), P()),
        out_specs=P("dp", "owner", None, None, None),
        check_vma=False,
    )
```

```python
import functools
import math

import jax
import jax.numpy as jnp
from jax import lax
from jax.experimental import pallas as pl
from jax.experimental.pallas import tpu as pltpu
from jax.sharding import PartitionSpec as P

f32, bf16 = jnp.float32, jnp.bfloat16
HIGHEST = lax.Precision.HIGHEST
AXES = ("dp", "owner")
CL_DEV = 8
PANEL = 64
GROUP = 16
ROWS_STEP = 512
MOVED = 32
STEPS = 4
TILE = 8
LEVELS = (24, 25, 28, 32)

IN_HBM = pl.BlockSpec(memory_space=pltpu.MemorySpace.HBM)


def dot(a, b, dims, precision=None):
    return lax.dot_general(a, b, (dims, ((), ())), precision=precision, preferred_element_type=f32)


def split(x):
    top = x.astype(bf16)
    return top, (x - top.astype(f32)).astype(bf16)


def grant(*order, room=24):
    return pltpu.CompilerParams(vmem_limit_bytes=room << 20, dimension_semantics=order or None)


def slots_kernel(capacity, ids_ref, out_ref, count_ref):
    blocks, width = ids_ref.shape
    clusters = count_ref.shape[1]
    names = lax.broadcasted_iota(jnp.int32, (clusters, width), 0)
    above = (
        lax.broadcasted_iota(jnp.int32, (width, width), 0)
        < lax.broadcasted_iota(jnp.int32, (width, width), 1)
    ).astype(bf16)
    count = jnp.zeros((clusters, 1), f32)
    count_ref[...] = jnp.zeros_like(count_ref)
    for block in range(blocks):
        hit = (names == ids_ref[block : block + 1, :]).astype(f32)
        before = dot(hit.astype(bf16), above, ((1,), (0,))) + count
        out_ref[block : block + 1, :] = jnp.sum(hit * before, axis=0, keepdims=True).astype(jnp.int32)
        count_ref[...] += dot(jnp.ones((8, width), bf16), hit.astype(bf16), ((1,), (1,)))
        count = count + jnp.sum(hit, axis=1, keepdims=True)
    tiles = jnp.broadcast_to(((count.astype(jnp.int32) + (TILE - 1)) // TILE).astype(f32), (clusters, width))
    later = lax.broadcasted_iota(jnp.int32, (clusters, clusters), 0)
    early = lax.broadcasted_iota(jnp.int32, (clusters, clusters), 1)
    ahead = (early < later) & (early // CL_DEV == later // CL_DEV)
    start = dot(ahead.astype(bf16), tiles.astype(bf16), ((1,), (0,))) * TILE
    start = start + (names // CL_DEV * (CL_DEV * capacity)).astype(f32)
    for block in range(blocks):
        hit = names == ids_ref[block : block + 1, :]
        first = jnp.sum(jnp.where(hit, start, 0.0), axis=0, keepdims=True)
        out_ref[block : block + 1, :] += first.astype(jnp.int32)


def slots(ids, clusters, capacity):
    rows = ids.shape[0]
    place, count = pl.pallas_call(
        functools.partial(slots_kernel, capacity),
        out_shape=(
            jax.ShapeDtypeStruct((rows // 128, 128), jnp.int32),
            jax.ShapeDtypeStruct((8, clusters), f32),
        ),
        cost_estimate=pl.CostEstimate(flops=1 << 30, bytes_accessed=1 << 22, transcendentals=0),
        name="slots",
    )(ids.reshape(rows // 128, 128))
    return place.reshape(rows), count


def moments_kernel(
    devices, emb_ref, start_hbm, cov_hbm, image_ref, mean_ref, total, cov_ref, start_ref, sems
):
    step = pl.program_id(0)
    width, n = start_ref.shape
    tile = min(256, width)
    load = pltpu.make_async_copy(start_hbm, start_ref, sems.at[0])
    save = pltpu.make_async_copy(cov_ref, cov_hbm, sems.at[1])

    @pl.when(step == 0)
    def _():
        load.start()
        total[...] = jnp.zeros_like(total)
        mean_ref[...] = jnp.zeros_like(mean_ref)

    rows = emb_ref[...]
    mean_ref[...] += jnp.sum(rows.astype(f32), axis=0, keepdims=True)
    for at in range(0, width, tile):
        total[at : at + tile, at:] += dot(rows[:, at : at + tile], rows[:, at:], ((0,), (0,)))

    @pl.when(step == pl.num_programs(0) - 1)
    def _():
        share = 1.0 / (rows.shape[0] * pl.num_programs(0))
        mean = mean_ref[...] * share
        mean_ref[...] = mean
        load.wait()
        start = start_ref[...]
        start_top, start_low = split(start)
        along = dot(mean, start, ((1,), (0,)), HIGHEST)
        mm = ((1,), (0,))
        down = [
            jnp.transpose(jnp.broadcast_to(mean[:, at : at + 128], (128, 128)))
            for at in range(0, width, 128)
        ]
        for at in range(0, width, 128):
            for to in range(at // tile * tile, width, 128):
                block = total[at : at + 128, to : to + 128] * share
                block = block - down[at // 128] * mean[:, to : to + 128]
                cov_ref[at : at + 128, to : to + 128] = block
                if to // tile != at // tile:
                    cov_ref[to : to + 128, at : at + 128] = jnp.transpose(block)
        save.start()
        piece = width // devices
        for at in range(0, width, 128):
            top, low = split(cov_ref[at : at + 128, :])
            image = dot(top, start_top, mm) + dot(top, start_low, mm) + dot(low, start_top, mm)
            for half in range(n // 128):
                part = image[:, half * 128 : half * 128 + 128]
                part = part + down[at // 128] * along[:, half * 128 : half * 128 + 128]
                for sub in range(128 // piece):
                    image_ref[at // piece + sub, half * piece : half * piece + piece, :] = part[
                        sub * piece : sub * piece + piece
                    ]
        extra = n // 128 * piece
        for row in range(width // 128):
            image_ref[:, extra + row : extra + row + 1, :] = jnp.broadcast_to(
                mean[:, row * 128 : row * 128 + 128][None], (devices, 1, 128)
            )
        save.wait()


def moments(emb, start, devices):
    rows, width = emb.shape
    n = start.shape[1]
    piece = width // devices
    step = rows // STEPS
    tall = n // 128 * piece + width // 128
    whole = lambda *shape: pl.BlockSpec(shape, lambda i: (0,) * len(shape))
    return pl.pallas_call(
        functools.partial(moments_kernel, devices),
        grid=(STEPS,),
        in_specs=[pl.BlockSpec((step, width), lambda i: (i, 0)), IN_HBM],
        out_specs=[IN_HBM, whole(devices, tall, 128), whole(1, width)],
        out_shape=[
            jax.ShapeDtypeStruct((width, width), f32),
            jax.ShapeDtypeStruct((devices, tall, 128), f32),
            jax.ShapeDtypeStruct((1, width), f32),
        ],
        scratch_shapes=[
            pltpu.VMEM((width, width), f32),
            pltpu.VMEM((width, width), f32),
            pltpu.VMEM((width, n), f32),
            pltpu.SemaphoreType.DMA((2,)),
        ],
        compiler_params=grant("arbitrary", room=56),
        name="moments",
    )(emb, start)


def basis_kernel(
    devices, side_ref, mine_ref, other_ref, mean_ref, here_ref, start_ref, cov_hbm,
    basis_ref, flip_ref, eigen_ref, image_at, aug, cov_ref, sem,
):
    load = pltpu.make_async_copy(cov_hbm, cov_ref, sem)
    load.start()
    width, n = start_ref.shape
    members, piece = mine_ref.shape[0], width // devices
    half = width // 2
    share = 1.0 / devices
    side = side_ref[0]
    for from_ref, at in ((mine_ref, side), (other_ref, 1 - side)):
        first = pl.multiple_of(at * half, half)
        for member in range(members):
            for part in range(n // 128):
                image_at[
                    pl.ds(first + member * piece, piece), part * 128 : part * 128 + 128
                ] = from_ref[member, part * piece : part * piece + piece, :]
    along = jnp.zeros((1, n), f32)
    for row in range(width // 128):
        along += dot(
            mean_ref[row : row + 1, :], start_ref[row * 128 : row * 128 + 128, :], ((1,), (0,)), HIGHEST
        )
    for row in range(width // 128):
        at = slice(row * 128, row * 128 + 128)
        down = jnp.transpose(jnp.broadcast_to(mean_ref[row : row + 1, :], (128, 128)))
        for part in range(0, n, 128):
            image_at[at, part : part + 128] = (
                image_at[at, part : part + 128] * share - down * along[:, part : part + 128]
            )
    image = image_at[...]
    aug[:, :n] = dot(image, image, ((0,), (0,)), HIGHEST)
    aug[:, n:] = (
        lax.broadcasted_iota(jnp.int32, (n, n), 0) == lax.broadcasted_iota(jnp.int32, (n, n), 1)
    ).astype(f32)
    eye = (
        lax.broadcasted_iota(jnp.int32, (PANEL, PANEL), 0)
        == lax.broadcasted_iota(jnp.int32, (PANEL, PANEL), 1)
    ).astype(f32)
    for first in range(0, n, PANEL):
        last = first + PANEL
        active = jnp.concatenate([aug[first:last, first:last], eye], axis=1)
        done = []
        for lead in range(0, PANEL, GROUP):
            row = lax.broadcasted_iota(jnp.int32, active.shape, 0)
            columns = [
                jnp.broadcast_to(active[:, lead + i : lead + i + 1], active.shape)
                for i in range(GROUP)
            ]
            pivots = [active[i : i + 1, :] for i in range(GROUP)]
            scale = jnp.zeros((GROUP, 2 * PANEL), f32)
            for i in range(GROUP):
                pivot = columns[i][i : i + 1, :]
                scale = jnp.where(row[:GROUP] == i, lax.rsqrt(pivot), scale)
                factor = jnp.where(row > i, columns[i] * (1.0 / pivot), 0.0)
                for j in range(i + 1, GROUP):
                    columns[j] = columns[j] - factor * columns[j][i : i + 1, :]
                for j in range(i + 1, GROUP):
                    pivots[j] = pivots[j] - factor[j : j + 1, :] * pivots[i]
                active = active - factor * pivots[i]
            done.append(active[:GROUP] * scale)
            active = active[GROUP:]
        inverse = jnp.concatenate(done, axis=0)[:, PANEL:]
        upper = dot(inverse, aug[first:last, :], ((1,), (0,)), HIGHEST)
        aug[first:last, :] = upper
        if last < n:
            aug[last:, :] = aug[last:, :] - dot(
                upper[:, last:n], upper, ((0,), (0,)), HIGHEST
            )
    basis = dot(image, aug[:, n:], ((1,), (1,)), HIGHEST)
    basis_ref[...] = basis
    basis_top, basis_low = split(basis)
    load.wait()
    cov_top, cov_low = split(cov_ref[...])
    mm = ((1,), (0,))
    curved = dot(cov_top, basis_top, mm) + dot(cov_top, basis_low, mm) + dot(cov_low, basis_top, mm)
    eigen = jnp.sum(basis * curved, axis=0, keepdims=True)
    apart = jnp.zeros((1, n), f32)
    for row in range(width // 128):
        off_here = here_ref[:, row * 128 : row * 128 + 128] - mean_ref[row : row + 1, :]
        apart += dot(off_here, basis_ref[row * 128 : row * 128 + 128, :], ((1,), (0,)), HIGHEST)
    eigen = (eigen + apart * apart) * share
    eigen_ref[...] = jnp.broadcast_to(eigen[None], eigen_ref.shape)
    signed = math.sqrt(width) * jnp.sum(basis, axis=0, keepdims=True)
    flip_ref[...] = signed / jnp.maximum(jnp.abs(signed), 1.0)


def basis_of(side, mine, other, mean, here, start, cov, devices):
    width, n = start.shape
    vmem = pl.BlockSpec(memory_space=pltpu.VMEM)
    return pl.pallas_call(
        functools.partial(basis_kernel, devices),
        in_specs=[pl.BlockSpec(memory_space=pltpu.SMEM)] + [vmem] * 5 + [IN_HBM],
        out_shape=(
            jax.ShapeDtypeStruct((width, n), f32),
            jax.ShapeDtypeStruct((1, n), f32),
            jax.ShapeDtypeStruct((devices, 1, n), f32),
        ),
        scratch_shapes=[
            pltpu.VMEM((width, n), f32),
            pltpu.VMEM((n, 2 * n), f32),
            pltpu.VMEM((width, width), f32),
            pltpu.SemaphoreType.DMA(()),
        ],
        compiler_params=grant(room=48),
        name="basis",
    )(side, mine, other, mean, here, start, cov)


def route_kernel(
    owners, dest_ref, me_ref, emb_ref, noise_ref, basis_ref, flip_ref, eigen_ref, mean_ref, *refs
):
    outs, (whiten, offset, fresh, slot) = refs[:owners], refs[owners:]
    step = pl.program_id(0)
    n = basis_ref.shape[1]
    parts = n // 128

    @pl.when(step == 0)
    def _():
        eigen = jnp.sum(eigen_ref[...], axis=0)
        whiten[...] = (basis_ref[...] * (flip_ref[...] / jnp.sqrt(eigen + 1e-06))).astype(bf16)
        shift = jnp.zeros((1, n), f32)
        for row in range(mean_ref.shape[0]):
            at = slice(row * 128, row * 128 + 128)
            shift += dot(mean_ref[row : row + 1, :], whiten[at, :].astype(f32), ((1,), (0,)), HIGHEST)
        offset[...] = shift

    values = dot(emb_ref[...], whiten[...], ((1,), (0,))) - offset[...] + noise_ref[...].astype(f32)
    for part in range(parts):
        fresh[part] = values[:, part * 128 : (part + 1) * 128]
    first = step * ROWS_STEP

    def move(group, carry):
        lead = group * MOVED
        ats = [dest_ref[first + lead + r] for r in range(MOVED)]
        for part in range(parts):
            rows = [fresh[part, pl.ds(lead + r, 1), :] for r in range(MOVED)]
            for at, row in zip(ats, rows):
                slot[part, pl.ds(at, 1), :] = row
        return carry

    lax.fori_loop(0, ROWS_STEP // MOVED, move, 0)

    @pl.when(step == pl.num_programs(0) - 1)
    def _():
        size, room = slot.shape[1] // owners, outs[0].shape[0]
        for k in range(owners):
            at = pl.multiple_of(lax.rem(me_ref[0] + k, owners) * size, size)
            for part in range(parts):
                outs[k][:, part * 128 : (part + 1) * 128] = slot[part, pl.ds(at, room), :].astype(bf16)


def route(dest, me, emb, noise, basis, flip, eigen, mean, owners, slot_count, room):
    rows, width = emb.shape
    n = basis.shape[1]
    whole = lambda array: pl.BlockSpec(array.shape, lambda i, *_: (0,) * array.ndim)
    return pl.pallas_call(
        functools.partial(route_kernel, owners),
        grid_spec=pltpu.PrefetchScalarGridSpec(
            num_scalar_prefetch=2,
            grid=(rows // ROWS_STEP,),
            in_specs=[
                pl.BlockSpec((ROWS_STEP, width), lambda i, *_: (i, 0)),
                pl.BlockSpec((ROWS_STEP, n), lambda i, *_: (i, 0)),
                whole(basis), whole(flip), whole(eigen), whole(mean),
            ],
            out_specs=[pl.BlockSpec((room, n), lambda i, *_: (0, 0))] * owners,
            scratch_shapes=[
                pltpu.VMEM((width, n), bf16),
                pltpu.VMEM((1, n), f32),
                pltpu.VMEM((n // 128, ROWS_STEP, 128), f32),
                pltpu.VMEM((n // 128, slot_count, 128), f32),
            ],
        ),
        out_shape=[jax.ShapeDtypeStruct((room, n), bf16)] * owners,
        compiler_params=grant("arbitrary"),
        name="route",
    )(dest, me, emb, noise, basis, flip, eigen, mean)


PART = 4


def unpack_kernel(capacity, source_ref, count_ref, block_ref, *refs):
    out_ref = refs[-1]
    lead = pl.program_id(0) * PART
    room, n = block_ref.shape
    base = source_ref[0] * CL_DEV
    tile = lax.fori_loop(
        0, lead, lambda c, at: at + (count_ref[base + c] + (TILE - 1)) // TILE, jnp.int32(0)
    )
    row = lax.broadcasted_iota(jnp.int32, (TILE, n), 0)
    for c in range(PART):
        count = count_ref[base + lead + c]
        for t in range(capacity // TILE):
            at = pl.multiple_of(jnp.minimum(tile + t, room // TILE - 1) * TILE, TILE)
            rows = block_ref[pl.ds(at, TILE), :]
            out_ref[c, 0, t * TILE : t * TILE + TILE, :] = jnp.where(
                row < count - t * TILE, rows, jnp.zeros_like(rows)
            )
        tile = tile + (count + (TILE - 1)) // TILE


def unpack(source, counts, block, arrived, owners, capacity):
    room, n = block.shape
    spec = pl.BlockSpec((PART, 1, capacity, n), lambda i, source_ref, *_: (i, source_ref[0], 0, 0))
    extra = [] if arrived is None else [arrived]
    return pl.pallas_call(
        functools.partial(unpack_kernel, capacity),
        grid_spec=pltpu.PrefetchScalarGridSpec(
            num_scalar_prefetch=2,
            grid=(CL_DEV // PART,),
            in_specs=[pl.BlockSpec((room, n), lambda i, *_: (0, 0))]
            + [pl.BlockSpec(memory_space=pl.ANY)] * len(extra),
            out_specs=spec,
        ),
        out_shape=jax.ShapeDtypeStruct((CL_DEV, owners, capacity, n), bf16),
        input_output_aliases={3: 0} if extra else {},
        compiler_params=grant("arbitrary"),
        cost_estimate=pl.CostEstimate(flops=1 << 20, bytes_accessed=1 << 20, transcendentals=0),
        name="unpack",
    )(source, counts, block, *extra)


def swap_pairs(block):
    return lax.ppermute(block, "dp", [(i, i ^ 1) for i in range(lax.axis_size("dp"))])


def exchange(blocks, groups=None):
    return lax.all_to_all(
        blocks, AXES, split_axis=0, concat_axis=0, tiled=True, axis_index_groups=groups
    )


def shards(embeddings, cluster_ids, noise, start_basis):
    rows_dev, width = embeddings.shape
    n = start_basis.shape[1]
    dp_size, owners = lax.axis_size("dp"), lax.axis_size("owner")
    devices = dp_size * owners
    clusters = CL_DEV * owners
    capacity = 2 * rows_dev // clusters
    place, count = slots(cluster_ids[:, 0], clusters, capacity)
    count = jnp.pad(count, ((0, 0), (0, -clusters % 128)))
    covariance, parts, mean_here = moments(embeddings, start_basis, devices)

    groups = [
        [d * owners + o for d in range(side, dp_size, 2) for o in range(owners)]
        for side in range(2)
    ]
    members = devices // 2
    side = lax.axis_index("dp") % 2
    keep = lax.dynamic_slice_in_dim(parts, side * members, members)
    send = lax.dynamic_slice_in_dim(parts, (1 - side) * members, members)
    piece = jnp.sum(exchange(keep + swap_pairs(send), groups), axis=0)
    tall = piece.shape[0] - width // 128
    mean = piece[tall:] / devices
    sent = jnp.concatenate([piece[:tall], count])
    mine = exchange(jnp.broadcast_to(sent[None], (members,) + sent.shape), groups)
    other = swap_pairs(mine)

    basis, flip, eigen = basis_of(
        side[None].astype(jnp.int32), mine, other, mean, mean_here, start_basis, covariance, devices
    )
    me = lax.axis_index("owner").astype(jnp.int32)
    tables = [t[:, tall, :clusters].astype(jnp.int32) for t in (mine, other)]
    rooms = [level * (CL_DEV * capacity) // 32 for level in LEVELS]
    need = jnp.int32(0)
    for table in tables:
        tiles = (table + (TILE - 1)) // TILE * TILE
        need = jnp.maximum(need, jnp.max(jnp.sum(tiles.reshape(members, owners, CL_DEV), axis=2)))
    level = jnp.sum((need > jnp.array(rooms[:-1], jnp.int32)).astype(jnp.int32))
    row_of = lax.axis_index("dp") // 2 * owners
    counts = lax.dynamic_slice(tables[0], (row_of, me * CL_DEV), (owners, CL_DEV)).reshape(-1)

    def deliver(room, place, me, embeddings, noise, basis, flip, eigen, mean, counts):
        blocks = route(
            place, me[None], embeddings, noise, basis, flip, eigen, mean,
            owners, clusters * capacity, room,
        )
        arrived = None
        for step in range(owners):
            block = blocks[step]
            if step:
                block = lax.ppermute(
                    block, "owner", [(i, (i + step) % owners) for i in range(owners)]
                )
            source = (me - step + owners) % owners
            arrived = unpack(source[None], counts, block, arrived, owners, capacity)
        return arrived

    arrived = lax.switch(
        level,
        [functools.partial(deliver, room) for room in rooms],
        place, me, embeddings, noise, basis, flip, exchange(eigen), mean, counts,
    )
    return arrived[None]


def solution(mesh):
    return jax.shard_map(
        shards,
        mesh=mesh,
        in_specs=(P(AXES, None), P(AXES, None), P(AXES, None), P()),
        out_specs=P("dp", "owner", None, None, None),
        check_vma=False,
    )
```

```python
import functools
import math

import jax
import jax.numpy as jnp
from jax import lax
from jax.experimental import pallas as pl
from jax.experimental.pallas import tpu as pltpu
from jax.sharding import PartitionSpec as P

f32, bf16 = jnp.float32, jnp.bfloat16
HIGHEST = lax.Precision.HIGHEST
AXES = ("dp", "owner")
CL_DEV = 8
PANEL = 64
GROUP = 16
ROWS_STEP = 512
MOVED = 32
STEPS = 4
TILE = 8
LEVELS = (47, 51, 55, 64)

IN_HBM = pl.BlockSpec(memory_space=pltpu.MemorySpace.HBM)


def dot(a, b, dims, precision=None):
    return lax.dot_general(a, b, (dims, ((), ())), precision=precision, preferred_element_type=f32)


def split(x):
    top = x.astype(bf16)
    return top, (x - top.astype(f32)).astype(bf16)


def grant(*order, room=24):
    return pltpu.CompilerParams(vmem_limit_bytes=room << 20, dimension_semantics=order or None)


def slots_kernel(capacity, ids_ref, out_ref, count_ref):
    blocks, width = ids_ref.shape
    clusters = count_ref.shape[1]
    names = lax.broadcasted_iota(jnp.int32, (clusters, width), 0)
    above = (
        lax.broadcasted_iota(jnp.int32, (width, width), 0)
        < lax.broadcasted_iota(jnp.int32, (width, width), 1)
    ).astype(bf16)
    count = jnp.zeros((clusters, 1), f32)
    count_ref[...] = jnp.zeros_like(count_ref)
    for block in range(blocks):
        hit = (names == ids_ref[block : block + 1, :]).astype(f32)
        before = dot(hit.astype(bf16), above, ((1,), (0,))) + count
        out_ref[block : block + 1, :] = jnp.sum(hit * before, axis=0, keepdims=True).astype(jnp.int32)
        count_ref[...] += dot(jnp.ones((8, width), bf16), hit.astype(bf16), ((1,), (1,)))
        count = count + jnp.sum(hit, axis=1, keepdims=True)
    tiles = jnp.broadcast_to(((count.astype(jnp.int32) + (TILE - 1)) // TILE).astype(f32), (clusters, width))
    later = lax.broadcasted_iota(jnp.int32, (clusters, clusters), 0)
    early = lax.broadcasted_iota(jnp.int32, (clusters, clusters), 1)
    ahead = (early < later) & (early // CL_DEV == later // CL_DEV)
    start = dot(ahead.astype(bf16), tiles.astype(bf16), ((1,), (0,))) * TILE
    start = start + (names // CL_DEV * (CL_DEV * capacity)).astype(f32)
    for block in range(blocks):
        hit = names == ids_ref[block : block + 1, :]
        first = jnp.sum(jnp.where(hit, start, 0.0), axis=0, keepdims=True)
        out_ref[block : block + 1, :] += first.astype(jnp.int32)


def slots(ids, clusters, capacity):
    rows = ids.shape[0]
    place, count = pl.pallas_call(
        functools.partial(slots_kernel, capacity),
        out_shape=(
            jax.ShapeDtypeStruct((rows // 128, 128), jnp.int32),
            jax.ShapeDtypeStruct((8, clusters), f32),
        ),
        cost_estimate=pl.CostEstimate(flops=1 << 30, bytes_accessed=1 << 22, transcendentals=0),
        name="slots",
    )(ids.reshape(rows // 128, 128))
    return place.reshape(rows), count


def moments_kernel(
    devices, side_ref, emb_ref, start_hbm, cov_hbm, keep_ref, send_ref, mean_ref,
    total, cov_ref, start_ref, image_ref, sems,
):
    step = pl.program_id(0)
    width, n = start_ref.shape
    tile = min(256, width)
    load = pltpu.make_async_copy(start_hbm, start_ref, sems.at[0])
    save = pltpu.make_async_copy(cov_ref, cov_hbm, sems.at[1])

    @pl.when(step == 0)
    def _():
        load.start()
        total[...] = jnp.zeros_like(total)
        mean_ref[...] = jnp.zeros_like(mean_ref)

    rows = emb_ref[...]
    mean_ref[...] += jnp.sum(rows.astype(f32), axis=0, keepdims=True)
    for at in range(0, width, tile):
        total[at : at + tile, at:] += dot(rows[:, at : at + tile], rows[:, at:], ((0,), (0,)))

    @pl.when(step == pl.num_programs(0) - 1)
    def _():
        share = 1.0 / (rows.shape[0] * pl.num_programs(0))
        mean = mean_ref[...] * share
        mean_ref[...] = mean
        load.wait()
        start = start_ref[...]
        start_top, start_low = split(start)
        along = dot(mean, start, ((1,), (0,)), HIGHEST)
        mm = ((1,), (0,))
        down = [
            jnp.transpose(jnp.broadcast_to(mean[:, at : at + 128], (128, 128)))
            for at in range(0, width, 128)
        ]
        for at in range(0, width, 128):
            for to in range(at // tile * tile, width, 128):
                block = total[at : at + 128, to : to + 128] * share
                block = block - down[at // 128] * mean[:, to : to + 128]
                cov_ref[at : at + 128, to : to + 128] = block
                if to // tile != at // tile:
                    cov_ref[to : to + 128, at : at + 128] = jnp.transpose(block)
        save.start()
        piece = width // devices
        for at in range(0, width, 128):
            top, low = split(cov_ref[at : at + 128, :])
            image = dot(top, start_top, mm) + dot(top, start_low, mm) + dot(low, start_top, mm)
            for half in range(n // 128):
                part = image[:, half * 128 : half * 128 + 128]
                part = part + down[at // 128] * along[:, half * 128 : half * 128 + 128]
                for sub in range(128 // piece):
                    image_ref[at // piece + sub, half * piece : half * piece + piece, :] = part[
                        sub * piece : sub * piece + piece
                    ]
        extra = n // 128 * piece
        for row in range(width // 128):
            image_ref[:, extra + row : extra + row + 1, :] = jnp.broadcast_to(
                mean[:, row * 128 : row * 128 + 128][None], (devices, 1, 128)
            )
        members = devices // 2
        keep_ref[...] = image_ref[pl.ds(side_ref[0] * members, members)]
        send_ref[...] = image_ref[pl.ds((1 - side_ref[0]) * members, members)]
        save.wait()


def moments(side, emb, start, devices):
    rows, width = emb.shape
    n = start.shape[1]
    tall = n // 128 * (width // devices) + width // 128
    half = (devices // 2, tall, 128)
    whole = lambda *shape: pl.BlockSpec(shape, lambda i, *_: (0,) * len(shape))
    return pl.pallas_call(
        functools.partial(moments_kernel, devices),
        grid_spec=pltpu.PrefetchScalarGridSpec(
            num_scalar_prefetch=1,
            grid=(STEPS,),
            in_specs=[pl.BlockSpec((rows // STEPS, width), lambda i, *_: (i, 0)), IN_HBM],
            out_specs=[IN_HBM, whole(*half), whole(*half), whole(1, width)],
            scratch_shapes=[
                pltpu.VMEM((width, width), f32),
                pltpu.VMEM((width, width), f32),
                pltpu.VMEM((width, n), f32),
                pltpu.VMEM((devices, tall, 128), f32),
                pltpu.SemaphoreType.DMA((2,)),
            ],
        ),
        out_shape=[
            jax.ShapeDtypeStruct((width, width), f32),
            jax.ShapeDtypeStruct(half, f32),
            jax.ShapeDtypeStruct(half, f32),
            jax.ShapeDtypeStruct((1, width), f32),
        ],
        compiler_params=grant("arbitrary", room=57),
        name="moments",
    )(side, emb, start)


def basis_kernel(
    devices, side_ref, mine_ref, other_ref, mean_ref, here_ref, start_ref, cov_hbm,
    basis_ref, flip_ref, eigen_ref, image_at, aug, cov_ref, turned, sem,
):
    load = pltpu.make_async_copy(cov_hbm, cov_ref, sem)
    load.start()
    width, n = start_ref.shape
    members, piece = mine_ref.shape[0], width // devices
    half = width // 2
    share = 1.0 / devices
    side = side_ref[0]
    for from_ref, at in ((mine_ref, side), (other_ref, 1 - side)):
        first = pl.multiple_of(at * half, half)
        for member in range(members):
            for part in range(n // 128):
                image_at[
                    pl.ds(first + member * piece, piece), part * 128 : part * 128 + 128
                ] = from_ref[member, part * piece : part * piece + piece, :]
    along = jnp.zeros((1, n), f32)
    for row in range(width // 128):
        along += dot(
            mean_ref[row : row + 1, :], start_ref[row * 128 : row * 128 + 128, :], ((1,), (0,)), HIGHEST
        )
    for row in range(width // 128):
        at = slice(row * 128, row * 128 + 128)
        down = jnp.transpose(jnp.broadcast_to(mean_ref[row : row + 1, :], (128, 128)))
        for part in range(0, n, 128):
            image_at[at, part : part + 128] = (
                image_at[at, part : part + 128] * share - down * along[:, part : part + 128]
            )
    image = image_at[...]
    aug[:, :n] = dot(image, image, ((0,), (0,)), HIGHEST)
    aug[:, n:] = (
        lax.broadcasted_iota(jnp.int32, (n, n), 0) == lax.broadcasted_iota(jnp.int32, (n, n), 1)
    ).astype(f32)
    eye = (
        lax.broadcasted_iota(jnp.int32, (PANEL, PANEL), 0)
        == lax.broadcasted_iota(jnp.int32, (PANEL, PANEL), 1)
    ).astype(f32)
    load.wait()
    cov_top, cov_low = split(cov_ref[...])
    image_top, image_low = split(image)
    mm = ((1,), (0,))
    turned[...] = (
        dot(cov_top, image_top, mm) + dot(cov_top, image_low, mm) + dot(cov_low, image_top, mm)
    )
    for first in range(0, n, PANEL):
        last = first + PANEL
        active = jnp.concatenate([aug[first:last, first:last], eye], axis=1)
        done = []
        for lead in range(0, PANEL, GROUP):
            row = lax.broadcasted_iota(jnp.int32, active.shape, 0)
            columns = [
                jnp.broadcast_to(active[:, lead + i : lead + i + 1], active.shape)
                for i in range(GROUP)
            ]
            pivots = [active[i : i + 1, :] for i in range(GROUP)]
            scale = jnp.zeros((GROUP, 2 * PANEL), f32)
            for i in range(GROUP):
                pivot = columns[i][i : i + 1, :]
                scale = jnp.where(row[:GROUP] == i, lax.rsqrt(pivot), scale)
                factor = jnp.where(row > i, columns[i] * (1.0 / pivot), 0.0)
                for j in range(i + 1, GROUP):
                    columns[j] = columns[j] - factor * columns[j][i : i + 1, :]
                for j in range(i + 1, GROUP):
                    pivots[j] = pivots[j] - factor[j : j + 1, :] * pivots[i]
                active = active - factor * pivots[i]
            done.append(active[:GROUP] * scale)
            active = active[GROUP:]
        inverse = jnp.concatenate(done, axis=0)[:, PANEL:]
        upper = dot(inverse, aug[first:last, :], ((1,), (0,)), HIGHEST)
        aug[first:last, :] = upper
        if last < n:
            aug[last:, :] = aug[last:, :] - dot(
                upper[:, last:n], upper, ((0,), (0,)), HIGHEST
            )
    basis = dot(image, aug[:, n:], ((1,), (1,)), HIGHEST)
    basis_ref[...] = basis
    turn_top, turn_low = split(aug[:, n:])
    turned_top, turned_low = split(turned[...])
    nt = ((1,), (1,))
    curved = dot(turned_top, turn_top, nt) + dot(turned_top, turn_low, nt) + dot(turned_low, turn_top, nt)
    eigen = jnp.sum(basis * curved, axis=0, keepdims=True)
    apart = jnp.zeros((1, n), f32)
    for row in range(width // 128):
        off_here = here_ref[:, row * 128 : row * 128 + 128] - mean_ref[row : row + 1, :]
        apart += dot(off_here, basis_ref[row * 128 : row * 128 + 128, :], ((1,), (0,)), HIGHEST)
    eigen = (eigen + apart * apart) * share
    eigen_ref[...] = jnp.broadcast_to(eigen[None], eigen_ref.shape)
    signed = math.sqrt(width) * jnp.sum(basis, axis=0, keepdims=True)
    flip_ref[...] = signed / jnp.maximum(jnp.abs(signed), 1.0)


def basis_of(side, mine, other, mean, here, start, cov, devices):
    width, n = start.shape
    vmem = pl.BlockSpec(memory_space=pltpu.VMEM)
    return pl.pallas_call(
        functools.partial(basis_kernel, devices),
        in_specs=[pl.BlockSpec(memory_space=pltpu.SMEM)] + [vmem] * 5 + [IN_HBM],
        out_shape=(
            jax.ShapeDtypeStruct((width, n), f32),
            jax.ShapeDtypeStruct((1, n), f32),
            jax.ShapeDtypeStruct((devices, 1, n), f32),
        ),
        scratch_shapes=[
            pltpu.VMEM((width, n), f32),
            pltpu.VMEM((n, 2 * n), f32),
            pltpu.VMEM((width, width), f32),
            pltpu.VMEM((width, n), f32),
            pltpu.SemaphoreType.DMA(()),
        ],
        compiler_params=grant(room=48),
        name="basis",
    )(side, mine, other, mean, here, start, cov)


def route_kernel(
    owners, dest_ref, me_ref, emb_ref, noise_ref, basis_ref, flip_ref, eigen_ref, mean_ref, *refs
):
    outs, (whiten, offset, fresh, slot) = refs[:owners], refs[owners:]
    step = pl.program_id(0)
    n = basis_ref.shape[1]
    parts = n // 128

    @pl.when(step == 0)
    def _():
        eigen = jnp.sum(eigen_ref[...], axis=0)
        whiten[...] = (basis_ref[...] * (flip_ref[...] / jnp.sqrt(eigen + 1e-06))).astype(bf16)
        shift = jnp.zeros((1, n), f32)
        for row in range(mean_ref.shape[0]):
            at = slice(row * 128, row * 128 + 128)
            shift += dot(mean_ref[row : row + 1, :], whiten[at, :].astype(f32), ((1,), (0,)), HIGHEST)
        offset[...] = shift

    values = dot(emb_ref[...], whiten[...], ((1,), (0,))) - offset[...] + noise_ref[...].astype(f32)
    for part in range(parts):
        fresh[part] = values[:, part * 128 : (part + 1) * 128]
    first = step * ROWS_STEP

    def move(group, carry):
        lead = group * MOVED
        ats = [dest_ref[first + lead + r] for r in range(MOVED)]
        for part in range(parts):
            rows = [fresh[part, pl.ds(lead + r, 1), :] for r in range(MOVED)]
            for at, row in zip(ats, rows):
                slot[part, pl.ds(at, 1), :] = row
        return carry

    lax.fori_loop(0, ROWS_STEP // MOVED, move, 0)

    @pl.when(step == pl.num_programs(0) - 1)
    def _():
        size, room = slot.shape[1] // owners, outs[0].shape[0]
        for k in range(owners):
            at = pl.multiple_of(lax.rem(me_ref[0] + k, owners) * size, size)
            for part in range(parts):
                outs[k][:, part * 128 : (part + 1) * 128] = slot[part, pl.ds(at, room), :].astype(bf16)


def route(dest, me, emb, noise, basis, flip, eigen, mean, owners, slot_count, room):
    rows, width = emb.shape
    n = basis.shape[1]
    whole = lambda array: pl.BlockSpec(array.shape, lambda i, *_: (0,) * array.ndim)
    return pl.pallas_call(
        functools.partial(route_kernel, owners),
        grid_spec=pltpu.PrefetchScalarGridSpec(
            num_scalar_prefetch=2,
            grid=(rows // ROWS_STEP,),
            in_specs=[
                pl.BlockSpec((ROWS_STEP, width), lambda i, *_: (i, 0)),
                pl.BlockSpec((ROWS_STEP, n), lambda i, *_: (i, 0)),
                whole(basis), whole(flip), whole(eigen), whole(mean),
            ],
            out_specs=[pl.BlockSpec((room, n), lambda i, *_: (0, 0))] * owners,
            scratch_shapes=[
                pltpu.VMEM((width, n), bf16),
                pltpu.VMEM((1, n), f32),
                pltpu.VMEM((n // 128, ROWS_STEP, 128), f32),
                pltpu.VMEM((n // 128, slot_count, 128), f32),
            ],
        ),
        out_shape=[jax.ShapeDtypeStruct((room, n), bf16)] * owners,
        compiler_params=grant("arbitrary"),
        name="route",
    )(dest, me, emb, noise, basis, flip, eigen, mean)


PART = 4


def unpack_kernel(capacity, source_ref, count_ref, block_ref, *refs):
    out_ref = refs[-1]
    lead = pl.program_id(0) * PART
    room, n = block_ref.shape
    base = source_ref[0] * CL_DEV
    tile = lax.fori_loop(
        0, lead, lambda c, at: at + (count_ref[base + c] + (TILE - 1)) // TILE, jnp.int32(0)
    )
    row = lax.broadcasted_iota(jnp.int32, (TILE, n), 0)
    for c in range(PART):
        count = count_ref[base + lead + c]
        for t in range(capacity // TILE):
            at = pl.multiple_of(jnp.minimum(tile + t, room // TILE - 1) * TILE, TILE)
            rows = block_ref[pl.ds(at, TILE), :]
            out_ref[c, 0, t * TILE : t * TILE + TILE, :] = jnp.where(
                row < count - t * TILE, rows, jnp.zeros_like(rows)
            )
        tile = tile + (count + (TILE - 1)) // TILE


def unpack(source, counts, block, arrived, owners, capacity):
    room, n = block.shape
    spec = pl.BlockSpec((PART, 1, capacity, n), lambda i, source_ref, *_: (i, source_ref[0], 0, 0))
    extra = [] if arrived is None else [arrived]
    return pl.pallas_call(
        functools.partial(unpack_kernel, capacity),
        grid_spec=pltpu.PrefetchScalarGridSpec(
            num_scalar_prefetch=2,
            grid=(CL_DEV // PART,),
            in_specs=[pl.BlockSpec((room, n), lambda i, *_: (0, 0))]
            + [pl.BlockSpec(memory_space=pl.ANY)] * len(extra),
            out_specs=spec,
        ),
        out_shape=jax.ShapeDtypeStruct((CL_DEV, owners, capacity, n), bf16),
        input_output_aliases={3: 0} if extra else {},
        compiler_params=grant("arbitrary"),
        cost_estimate=pl.CostEstimate(flops=1 << 20, bytes_accessed=1 << 20, transcendentals=0),
        name="unpack",
    )(source, counts, block, *extra)


def swap_pairs(block):
    return lax.ppermute(block, "dp", [(i, i ^ 1) for i in range(lax.axis_size("dp"))])


def exchange(blocks, groups=None):
    return lax.all_to_all(
        blocks, AXES, split_axis=0, concat_axis=0, tiled=True, axis_index_groups=groups
    )


def shards(embeddings, cluster_ids, noise, start_basis):
    rows_dev, width = embeddings.shape
    n = start_basis.shape[1]
    dp_size, owners = lax.axis_size("dp"), lax.axis_size("owner")
    devices = dp_size * owners
    clusters = CL_DEV * owners
    capacity = 2 * rows_dev // clusters
    place, count = slots(cluster_ids[:, 0], clusters, capacity)
    count = jnp.pad(count, ((0, 0), (0, -clusters % 128)))
    side = (lax.axis_index("dp") % 2).astype(jnp.int32)[None]
    covariance, keep, send, mean_here = moments(side, embeddings, start_basis, devices)

    groups = [
        [d * owners + o for d in range(side, dp_size, 2) for o in range(owners)]
        for side in range(2)
    ]
    members = devices // 2
    piece = jnp.sum(exchange(keep + swap_pairs(send), groups), axis=0)
    tall = piece.shape[0] - width // 128
    mean = piece[tall:] / devices
    sent = jnp.concatenate([piece[:tall], count])
    mine = exchange(jnp.broadcast_to(sent[None], (members,) + sent.shape), groups)
    other = swap_pairs(mine)

    basis, flip, eigen = basis_of(
        side, mine, other, mean, mean_here, start_basis, covariance, devices
    )
    me = lax.axis_index("owner").astype(jnp.int32)
    tables = [t[:, tall, :clusters].astype(jnp.int32) for t in (mine, other)]
    rooms = [level * (CL_DEV * capacity) // 64 for level in LEVELS]
    need = jnp.int32(0)
    for table in tables:
        tiles = (table + (TILE - 1)) // TILE * TILE
        need = jnp.maximum(need, jnp.max(jnp.sum(tiles.reshape(members, owners, CL_DEV), axis=2)))
    level = jnp.sum((need > jnp.array(rooms[:-1], jnp.int32)).astype(jnp.int32))
    row_of = lax.axis_index("dp") // 2 * owners
    counts = lax.dynamic_slice(tables[0], (row_of, me * CL_DEV), (owners, CL_DEV)).reshape(-1)

    def deliver(room, place, me, embeddings, noise, basis, flip, eigen, mean, counts):
        blocks = route(
            place, me[None], embeddings, noise, basis, flip, eigen, mean,
            owners, clusters * capacity, room,
        )
        arrived = None
        for step in range(owners):
            block = blocks[step]
            if step:
                block = lax.ppermute(
                    block, "owner", [(i, (i + step) % owners) for i in range(owners)]
                )
            source = (me - step + owners) % owners
            arrived = unpack(source[None], counts, block, arrived, owners, capacity)
        return arrived

    arrived = lax.switch(
        level,
        [functools.partial(deliver, room) for room in rooms],
        place, me, embeddings, noise, basis, flip, exchange(eigen), mean, counts,
    )
    return arrived[None]


def solution(mesh):
    return jax.shard_map(
        shards,
        mesh=mesh,
        in_specs=(P(AXES, None), P(AXES, None), P(AXES, None), P()),
        out_specs=P("dp", "owner", None, None, None),
        check_vma=False,
    )
```

```python
import functools
import math

import jax
import jax.numpy as jnp
from jax import lax
from jax.experimental import pallas as pl
from jax.experimental.pallas import tpu as pltpu
from jax.sharding import PartitionSpec as P

f32, bf16 = jnp.float32, jnp.bfloat16
HIGHEST = lax.Precision.HIGHEST
AXES = ("dp", "owner")
CL_DEV = 8
PANEL = 64
GROUP = 16
ROWS_STEP = 512
MOVED = 32
STEPS = 4
TILE = 8
LEVELS = (46, 49, 52, 56, 64)

IN_HBM = pl.BlockSpec(memory_space=pltpu.MemorySpace.HBM)


def dot(a, b, dims, precision=None):
    return lax.dot_general(a, b, (dims, ((), ())), precision=precision, preferred_element_type=f32)


def split(x):
    top = x.astype(bf16)
    return top, (x - top.astype(f32)).astype(bf16)


def stand(row):
    return jnp.transpose(jnp.broadcast_to(row, (128, 128)))


def weigh(downs, table):
    sums = []
    for part in range(0, table.shape[1], 128):
        total = jnp.zeros((128, 128), f32)
        for index, down in enumerate(downs):
            total = total + down * table[index * 128 : index * 128 + 128, part : part + 128].astype(f32)
        sums.append(jnp.sum(total, axis=0, keepdims=True))
    return jnp.concatenate(sums, axis=1)


def grant(*order, room=24):
    return pltpu.CompilerParams(vmem_limit_bytes=room << 20, dimension_semantics=order or None)


def slots_kernel(capacity, ids_ref, out_ref, count_ref):
    blocks, width = ids_ref.shape
    clusters = count_ref.shape[1]
    names = lax.broadcasted_iota(jnp.int32, (clusters, width), 0)
    above = (
        lax.broadcasted_iota(jnp.int32, (width, width), 0)
        < lax.broadcasted_iota(jnp.int32, (width, width), 1)
    ).astype(bf16)
    count = jnp.zeros((clusters, 1), f32)
    count_ref[...] = jnp.zeros_like(count_ref)
    for block in range(blocks):
        hit = (names == ids_ref[block : block + 1, :]).astype(f32)
        before = dot(hit.astype(bf16), above, ((1,), (0,))) + count
        out_ref[block : block + 1, :] = jnp.sum(hit * before, axis=0, keepdims=True).astype(jnp.int32)
        count_ref[...] += dot(jnp.ones((8, width), bf16), hit.astype(bf16), ((1,), (1,)))
        count = count + jnp.sum(hit, axis=1, keepdims=True)
    tiles = jnp.broadcast_to(((count.astype(jnp.int32) + (TILE - 1)) // TILE).astype(f32), (clusters, width))
    later = lax.broadcasted_iota(jnp.int32, (clusters, clusters), 0)
    early = lax.broadcasted_iota(jnp.int32, (clusters, clusters), 1)
    ahead = (early < later) & (early // CL_DEV == later // CL_DEV)
    start = dot(ahead.astype(bf16), tiles.astype(bf16), ((1,), (0,))) * TILE
    start = start + (names // CL_DEV * (CL_DEV * capacity)).astype(f32)
    for block in range(blocks):
        hit = names == ids_ref[block : block + 1, :]
        first = jnp.sum(jnp.where(hit, start, 0.0), axis=0, keepdims=True)
        out_ref[block : block + 1, :] += first.astype(jnp.int32)


def slots(ids, clusters, capacity):
    rows = ids.shape[0]
    place, count = pl.pallas_call(
        functools.partial(slots_kernel, capacity),
        out_shape=(
            jax.ShapeDtypeStruct((rows // 128, 128), jnp.int32),
            jax.ShapeDtypeStruct((8, clusters), f32),
        ),
        cost_estimate=pl.CostEstimate(flops=1 << 30, bytes_accessed=1 << 22, transcendentals=0),
        name="slots",
    )(ids.reshape(rows // 128, 128))
    return place.reshape(rows), count


def moments_kernel(
    devices, side_ref, emb_ref, start_hbm, cov_hbm, keep_ref, send_ref, mean_ref,
    total, cov_ref, start_ref, image_ref, sems,
):
    step = pl.program_id(0)
    width, n = start_ref.shape
    tile = min(256, width)
    load = pltpu.make_async_copy(start_hbm, start_ref, sems.at[0])
    save = pltpu.make_async_copy(cov_ref, cov_hbm, sems.at[1])

    @pl.when(step == 0)
    def _():
        load.start()
        total[...] = jnp.zeros_like(total)
        mean_ref[...] = jnp.zeros_like(mean_ref)

    rows = emb_ref[...]
    mean_ref[...] += jnp.sum(rows.astype(f32), axis=0, keepdims=True)
    for at in range(0, width, tile):
        total[at : at + tile, at:] += dot(rows[:, at : at + tile], rows[:, at:], ((0,), (0,)))

    @pl.when(step == pl.num_programs(0) - 1)
    def _():
        share = 1.0 / (rows.shape[0] * pl.num_programs(0))
        mean = mean_ref[...] * share
        mean_ref[...] = mean
        load.wait()
        start = start_ref[...]
        start_top, start_low = split(start)
        mm = ((1,), (0,))
        down = [stand(mean[:, at : at + 128]) for at in range(0, width, 128)]
        along = weigh(down, start)
        for at in range(0, width, 128):
            for to in range(at // tile * tile, width, 128):
                block = total[at : at + 128, to : to + 128] * share
                block = block - down[at // 128] * mean[:, to : to + 128]
                cov_ref[at : at + 128, to : to + 128] = block
                if to // tile != at // tile:
                    cov_ref[to : to + 128, at : at + 128] = jnp.transpose(block)
        save.start()
        piece = width // devices
        for at in range(0, width, 128):
            top, low = split(cov_ref[at : at + 128, :])
            image = dot(top, start_top, mm) + dot(top, start_low, mm) + dot(low, start_top, mm)
            for half in range(n // 128):
                part = image[:, half * 128 : half * 128 + 128]
                part = part + down[at // 128] * along[:, half * 128 : half * 128 + 128]
                for sub in range(128 // piece):
                    image_ref[at // piece + sub, half * piece : half * piece + piece, :] = part[
                        sub * piece : sub * piece + piece
                    ]
        extra = n // 128 * piece
        for row in range(width // 128):
            image_ref[:, extra + row : extra + row + 1, :] = jnp.broadcast_to(
                mean[:, row * 128 : row * 128 + 128][None], (devices, 1, 128)
            )
        members = devices // 2
        keep_ref[...] = image_ref[pl.ds(side_ref[0] * members, members)]
        send_ref[...] = image_ref[pl.ds((1 - side_ref[0]) * members, members)]
        save.wait()


def moments(side, emb, start, devices):
    rows, width = emb.shape
    n = start.shape[1]
    tall = n // 128 * (width // devices) + width // 128
    half = (devices // 2, tall, 128)
    whole = lambda *shape: pl.BlockSpec(shape, lambda i, *_: (0,) * len(shape))
    return pl.pallas_call(
        functools.partial(moments_kernel, devices),
        grid_spec=pltpu.PrefetchScalarGridSpec(
            num_scalar_prefetch=1,
            grid=(STEPS,),
            in_specs=[pl.BlockSpec((rows // STEPS, width), lambda i, *_: (i, 0)), IN_HBM],
            out_specs=[IN_HBM, whole(*half), whole(*half), whole(1, width)],
            scratch_shapes=[
                pltpu.VMEM((width, width), f32),
                pltpu.VMEM((width, width), f32),
                pltpu.VMEM((width, n), f32),
                pltpu.VMEM((devices, tall, 128), f32),
                pltpu.SemaphoreType.DMA((2,)),
            ],
        ),
        out_shape=[
            jax.ShapeDtypeStruct((width, width), f32),
            jax.ShapeDtypeStruct(half, f32),
            jax.ShapeDtypeStruct(half, f32),
            jax.ShapeDtypeStruct((1, width), f32),
        ],
        compiler_params=grant("arbitrary", room=50),
        name="moments",
    )(side, emb, start)


def basis_kernel(
    devices, side_ref, mine_ref, other_ref, mean_ref, here_ref, start_ref, cov_hbm,
    basis_ref, flip_ref, eigen_ref, image_at, aug, cov_ref, turned, sem,
):
    load = pltpu.make_async_copy(cov_hbm, cov_ref, sem)
    load.start()
    width, n = start_ref.shape
    members, piece = mine_ref.shape[0], width // devices
    half = width // 2
    share = 1.0 / devices
    side = side_ref[0]
    for from_ref, at in ((mine_ref, side), (other_ref, 1 - side)):
        first = pl.multiple_of(at * half, half)
        for member in range(members):
            for part in range(n // 128):
                image_at[
                    pl.ds(first + member * piece, piece), part * 128 : part * 128 + 128
                ] = from_ref[member, part * piece : part * piece + piece, :]
    downs = [stand(mean_ref[row : row + 1, :]) for row in range(width // 128)]
    along = weigh(downs, start_ref)
    for row, down in enumerate(downs):
        at = slice(row * 128, row * 128 + 128)
        for part in range(0, n, 128):
            image_at[at, part : part + 128] = (
                image_at[at, part : part + 128] * share - down * along[:, part : part + 128]
            )
    image = image_at[...]
    aug[:, :n] = dot(image, image, ((0,), (0,)), HIGHEST)
    aug[:, n:] = (
        lax.broadcasted_iota(jnp.int32, (n, n), 0) == lax.broadcasted_iota(jnp.int32, (n, n), 1)
    ).astype(f32)
    eye = (
        lax.broadcasted_iota(jnp.int32, (PANEL, PANEL), 0)
        == lax.broadcasted_iota(jnp.int32, (PANEL, PANEL), 1)
    ).astype(f32)
    load.wait()
    cov_top, cov_low = split(cov_ref[...])
    image_top, image_low = split(image)
    mm = ((1,), (0,))
    turned[...] = (
        dot(cov_top, image_top, mm) + dot(cov_top, image_low, mm) + dot(cov_low, image_top, mm)
    )
    for first in range(0, n, PANEL):
        last = first + PANEL
        active = jnp.concatenate([aug[first:last, first:last], eye], axis=1)
        done = []
        for lead in range(0, PANEL, GROUP):
            row = lax.broadcasted_iota(jnp.int32, active.shape, 0)
            columns = [
                jnp.broadcast_to(active[:, lead + i : lead + i + 1], active.shape)
                for i in range(GROUP)
            ]
            pivots = [active[i : i + 1, :] for i in range(GROUP)]
            scale = jnp.zeros((GROUP, 2 * PANEL), f32)
            for i in range(GROUP):
                pivot = columns[i][i : i + 1, :]
                scale = jnp.where(row[:GROUP] == i, lax.rsqrt(pivot), scale)
                factor = jnp.where(row > i, columns[i] * (1.0 / pivot), 0.0)
                for j in range(i + 1, GROUP):
                    columns[j] = columns[j] - factor * columns[j][i : i + 1, :]
                for j in range(i + 1, GROUP):
                    pivots[j] = pivots[j] - factor[j : j + 1, :] * pivots[i]
                active = active - factor * pivots[i]
            done.append(active[:GROUP] * scale)
            active = active[GROUP:]
        inverse = jnp.concatenate(done, axis=0)[:, PANEL:]
        upper = dot(inverse, aug[first:last, :], ((1,), (0,)), HIGHEST)
        aug[first:last, :] = upper
        if last < n:
            aug[last:, :] = aug[last:, :] - dot(
                upper[:, last:n], upper, ((0,), (0,)), HIGHEST
            )
    basis = dot(image, aug[:, n:], ((1,), (1,)), HIGHEST)
    basis_ref[...] = basis
    turn_top, turn_low = split(aug[:, n:])
    turned_top, turned_low = split(turned[...])
    nt = ((1,), (1,))
    curved = dot(turned_top, turn_top, nt) + dot(turned_top, turn_low, nt) + dot(turned_low, turn_top, nt)
    eigen = jnp.sum(basis * curved, axis=0, keepdims=True)
    apart = weigh(
        [
            stand(here_ref[:, row * 128 : row * 128 + 128] - mean_ref[row : row + 1, :])
            for row in range(width // 128)
        ],
        basis,
    )
    eigen = (eigen + apart * apart) * share
    eigen_ref[...] = jnp.broadcast_to(eigen[None], eigen_ref.shape)
    signed = math.sqrt(width) * jnp.sum(basis, axis=0, keepdims=True)
    flip_ref[...] = signed / jnp.maximum(jnp.abs(signed), 1.0)


def basis_of(side, mine, other, mean, here, start, cov, devices):
    width, n = start.shape
    vmem = pl.BlockSpec(memory_space=pltpu.VMEM)
    return pl.pallas_call(
        functools.partial(basis_kernel, devices),
        in_specs=[pl.BlockSpec(memory_space=pltpu.SMEM)] + [vmem] * 5 + [IN_HBM],
        out_shape=(
            jax.ShapeDtypeStruct((width, n), f32),
            jax.ShapeDtypeStruct((1, n), f32),
            jax.ShapeDtypeStruct((devices, 1, n), f32),
        ),
        scratch_shapes=[
            pltpu.VMEM((width, n), f32),
            pltpu.VMEM((n, 2 * n), f32),
            pltpu.VMEM((width, width), f32),
            pltpu.VMEM((width, n), f32),
            pltpu.SemaphoreType.DMA(()),
        ],
        compiler_params=grant(room=48),
        name="basis",
    )(side, mine, other, mean, here, start, cov)


def route_kernel(
    owners, dest_ref, me_ref, emb_ref, noise_ref, basis_ref, flip_ref, eigen_ref, mean_ref, *refs
):
    outs, (whiten, offset, fresh, slot) = refs[:owners], refs[owners:]
    step = pl.program_id(0)
    n = basis_ref.shape[1]
    parts = n // 128

    @pl.when(step == 0)
    def _():
        eigen = jnp.sum(eigen_ref[...], axis=0)
        whiten[...] = (basis_ref[...] * (flip_ref[...] / jnp.sqrt(eigen + 1e-06))).astype(bf16)
        offset[...] = weigh(
            [stand(mean_ref[row : row + 1, :]) for row in range(mean_ref.shape[0])], whiten
        )

    values = dot(emb_ref[...], whiten[...], ((1,), (0,))) - offset[...] + noise_ref[...].astype(f32)
    for part in range(parts):
        fresh[part] = values[:, part * 128 : (part + 1) * 128]
    first = step * ROWS_STEP

    def move(group, carry):
        lead = group * MOVED
        ats = [dest_ref[first + lead + r] for r in range(MOVED)]
        for part in range(parts):
            rows = [fresh[part, pl.ds(lead + r, 1), :] for r in range(MOVED)]
            for at, row in zip(ats, rows):
                slot[part, pl.ds(at, 1), :] = row
        return carry

    lax.fori_loop(0, ROWS_STEP // MOVED, move, 0)

    @pl.when(step == pl.num_programs(0) - 1)
    def _():
        size, room = slot.shape[1] // owners, outs[0].shape[0]
        for k in range(owners):
            at = pl.multiple_of(lax.rem(me_ref[0] + k, owners) * size, size)
            for part in range(parts):
                outs[k][:, part * 128 : (part + 1) * 128] = slot[part, pl.ds(at, room), :].astype(bf16)


def route(dest, me, emb, noise, basis, flip, eigen, mean, owners, slot_count, room):
    rows, width = emb.shape
    n = basis.shape[1]
    whole = lambda array: pl.BlockSpec(array.shape, lambda i, *_: (0,) * array.ndim)
    return pl.pallas_call(
        functools.partial(route_kernel, owners),
        grid_spec=pltpu.PrefetchScalarGridSpec(
            num_scalar_prefetch=2,
            grid=(rows // ROWS_STEP,),
            in_specs=[
                pl.BlockSpec((ROWS_STEP, width), lambda i, *_: (i, 0)),
                pl.BlockSpec((ROWS_STEP, n), lambda i, *_: (i, 0)),
                whole(basis), whole(flip), whole(eigen), whole(mean),
            ],
            out_specs=[pl.BlockSpec((room, n), lambda i, *_: (0, 0))] * owners,
            scratch_shapes=[
                pltpu.VMEM((width, n), bf16),
                pltpu.VMEM((1, n), f32),
                pltpu.VMEM((n // 128, ROWS_STEP, 128), f32),
                pltpu.VMEM((n // 128, slot_count, 128), f32),
            ],
        ),
        out_shape=[jax.ShapeDtypeStruct((room, n), bf16)] * owners,
        compiler_params=grant("arbitrary"),
        name="route",
    )(dest, me, emb, noise, basis, flip, eigen, mean)


PART = 4


def unpack_kernel(capacity, source_ref, count_ref, block_ref, *refs):
    out_ref = refs[-1]
    lead = pl.program_id(0) * PART
    room, n = block_ref.shape
    base = source_ref[0] * CL_DEV
    tile = lax.fori_loop(
        0, lead, lambda c, at: at + (count_ref[base + c] + (TILE - 1)) // TILE, jnp.int32(0)
    )
    row = lax.broadcasted_iota(jnp.int32, (TILE, n), 0)
    for c in range(PART):
        count = count_ref[base + lead + c]
        for t in range(capacity // TILE):
            at = pl.multiple_of(jnp.minimum(tile + t, room // TILE - 1) * TILE, TILE)
            rows = block_ref[pl.ds(at, TILE), :]
            out_ref[c, 0, t * TILE : t * TILE + TILE, :] = jnp.where(
                row < count - t * TILE, rows, jnp.zeros_like(rows)
            )
        tile = tile + (count + (TILE - 1)) // TILE


def unpack(source, counts, block, arrived, owners, capacity):
    room, n = block.shape
    spec = pl.BlockSpec((PART, 1, capacity, n), lambda i, source_ref, *_: (i, source_ref[0], 0, 0))
    extra = [] if arrived is None else [arrived]
    return pl.pallas_call(
        functools.partial(unpack_kernel, capacity),
        grid_spec=pltpu.PrefetchScalarGridSpec(
            num_scalar_prefetch=2,
            grid=(CL_DEV // PART,),
            in_specs=[pl.BlockSpec((room, n), lambda i, *_: (0, 0))]
            + [pl.BlockSpec(memory_space=pl.ANY)] * len(extra),
            out_specs=spec,
        ),
        out_shape=jax.ShapeDtypeStruct((CL_DEV, owners, capacity, n), bf16),
        input_output_aliases={3: 0} if extra else {},
        compiler_params=grant("arbitrary"),
        cost_estimate=pl.CostEstimate(flops=1 << 20, bytes_accessed=1 << 20, transcendentals=0),
        name="unpack",
    )(source, counts, block, *extra)


def swap_pairs(block):
    return lax.ppermute(block, "dp", [(i, i ^ 1) for i in range(lax.axis_size("dp"))])


def exchange(blocks, groups=None):
    return lax.all_to_all(
        blocks, AXES, split_axis=0, concat_axis=0, tiled=True, axis_index_groups=groups
    )


def shards(embeddings, cluster_ids, noise, start_basis):
    rows_dev, width = embeddings.shape
    n = start_basis.shape[1]
    dp_size, owners = lax.axis_size("dp"), lax.axis_size("owner")
    devices = dp_size * owners
    clusters = CL_DEV * owners
    capacity = 2 * rows_dev // clusters
    place, count = slots(cluster_ids[:, 0], clusters, capacity)
    count = jnp.pad(count, ((0, 0), (0, -clusters % 128)))
    side = (lax.axis_index("dp") % 2).astype(jnp.int32)[None]
    covariance, keep, send, mean_here = moments(side, embeddings, start_basis, devices)

    groups = [
        [d * owners + o for d in range(side, dp_size, 2) for o in range(owners)]
        for side in range(2)
    ]
    members = devices // 2
    piece = jnp.sum(exchange(keep + swap_pairs(send), groups), axis=0)
    tall = piece.shape[0] - width // 128
    mean = piece[tall:] / devices
    sent = jnp.concatenate([piece[:tall], count])
    mine = exchange(jnp.broadcast_to(sent[None], (members,) + sent.shape), groups)
    other = swap_pairs(mine)

    basis, flip, eigen = basis_of(
        side, mine, other, mean, mean_here, start_basis, covariance, devices
    )
    me = lax.axis_index("owner").astype(jnp.int32)
    tables = [t[:, tall, :clusters].astype(jnp.int32) for t in (mine, other)]
    rooms = [level * (CL_DEV * capacity) // 64 for level in LEVELS]
    need = jnp.int32(0)
    for table in tables:
        tiles = (table + (TILE - 1)) // TILE * TILE
        need = jnp.maximum(need, jnp.max(jnp.sum(tiles.reshape(members, owners, CL_DEV), axis=2)))
    level = jnp.sum((need > jnp.array(rooms[:-1], jnp.int32)).astype(jnp.int32))
    row_of = lax.axis_index("dp") // 2 * owners
    counts = lax.dynamic_slice(tables[0], (row_of, me * CL_DEV), (owners, CL_DEV)).reshape(-1)

    def deliver(room, place, me, embeddings, noise, basis, flip, eigen, mean, counts):
        blocks = route(
            place, me[None], embeddings, noise, basis, flip, eigen, mean,
            owners, clusters * capacity, room,
        )
        arrived = None
        for step in range(owners):
            block = blocks[step]
            if step:
                block = lax.ppermute(
                    block, "owner", [(i, (i + step) % owners) for i in range(owners)]
                )
            source = (me - step + owners) % owners
            arrived = unpack(source[None], counts, block, arrived, owners, capacity)
        return arrived

    arrived = lax.switch(
        level,
        [functools.partial(deliver, room) for room in rooms],
        place, me, embeddings, noise, basis, flip, exchange(eigen), mean, counts,
    )
    return arrived[None]


def solution(mesh):
    return jax.shard_map(
        shards,
        mesh=mesh,
        in_specs=(P(AXES, None), P(AXES, None), P(AXES, None), P()),
        out_specs=P("dp", "owner", None, None, None),
        check_vma=False,
    )
```

```python
import functools
import math

import jax
import jax.numpy as jnp
from jax import lax
from jax.experimental import pallas as pl
from jax.experimental.pallas import tpu as pltpu
from jax.sharding import PartitionSpec as P

f32, bf16 = jnp.float32, jnp.bfloat16
HIGHEST = lax.Precision.HIGHEST
AXES = ("dp", "owner")
CL_DEV = 8
PANEL = 64
GROUP = 16
ROWS_STEP = 512
MOVED = 32
STEPS = 4
TILE = 8
LEVELS = (46, 49, 52, 56, 64)

IN_HBM = pl.BlockSpec(memory_space=pltpu.MemorySpace.HBM)


def dot(a, b, dims, precision=None):
    return lax.dot_general(a, b, (dims, ((), ())), precision=precision, preferred_element_type=f32)


def split(x):
    top = x.astype(bf16)
    return top, (x - top.astype(f32)).astype(bf16)


def stand(row):
    return jnp.transpose(jnp.broadcast_to(row, (128, 128)))


def weigh(downs, table):
    sums = []
    for part in range(0, table.shape[1], 128):
        total = jnp.zeros((128, 128), f32)
        for index, down in enumerate(downs):
            total = total + down * table[index * 128 : index * 128 + 128, part : part + 128].astype(f32)
        sums.append(jnp.sum(total, axis=0, keepdims=True))
    return jnp.concatenate(sums, axis=1)


def grant(*order, room=24):
    return pltpu.CompilerParams(vmem_limit_bytes=room << 20, dimension_semantics=order or None)


def slots_kernel(capacity, ids_ref, out_ref, count_ref):
    blocks, width = ids_ref.shape
    clusters = count_ref.shape[1]
    names = lax.broadcasted_iota(jnp.int32, (clusters, width), 0)
    above = (
        lax.broadcasted_iota(jnp.int32, (width, width), 0)
        < lax.broadcasted_iota(jnp.int32, (width, width), 1)
    ).astype(bf16)
    count = jnp.zeros((clusters, 1), f32)
    count_ref[...] = jnp.zeros_like(count_ref)
    for block in range(blocks):
        hit = (names == ids_ref[block : block + 1, :]).astype(f32)
        before = dot(hit.astype(bf16), above, ((1,), (0,))) + count
        out_ref[block : block + 1, :] = jnp.sum(hit * before, axis=0, keepdims=True).astype(jnp.int32)
        count_ref[...] += dot(jnp.ones((8, width), bf16), hit.astype(bf16), ((1,), (1,)))
        count = count + jnp.sum(hit, axis=1, keepdims=True)
    tiles = jnp.broadcast_to(((count.astype(jnp.int32) + (TILE - 1)) // TILE).astype(f32), (clusters, width))
    later = lax.broadcasted_iota(jnp.int32, (clusters, clusters), 0)
    early = lax.broadcasted_iota(jnp.int32, (clusters, clusters), 1)
    ahead = (early < later) & (early // CL_DEV == later // CL_DEV)
    start = dot(ahead.astype(bf16), tiles.astype(bf16), ((1,), (0,))) * TILE
    start = start + (names // CL_DEV * (CL_DEV * capacity)).astype(f32)
    for block in range(blocks):
        hit = names == ids_ref[block : block + 1, :]
        first = jnp.sum(jnp.where(hit, start, 0.0), axis=0, keepdims=True)
        out_ref[block : block + 1, :] += first.astype(jnp.int32)


def slots(ids, clusters, capacity):
    rows = ids.shape[0]
    place, count = pl.pallas_call(
        functools.partial(slots_kernel, capacity),
        out_shape=(
            jax.ShapeDtypeStruct((rows // 128, 128), jnp.int32),
            jax.ShapeDtypeStruct((8, clusters), f32),
        ),
        cost_estimate=pl.CostEstimate(flops=1 << 30, bytes_accessed=1 << 22, transcendentals=0),
        name="slots",
    )(ids.reshape(rows // 128, 128))
    return place.reshape(rows), count


def moments_kernel(
    devices, side_ref, emb_ref, start_hbm, cov_hbm, keep_ref, send_ref, mean_ref,
    total, cov_ref, start_ref, image_ref, sems,
):
    step = pl.program_id(0)
    width, n = start_ref.shape
    tile = min(256, width)
    load = pltpu.make_async_copy(start_hbm, start_ref, sems.at[0])
    save = pltpu.make_async_copy(cov_ref, cov_hbm, sems.at[1])

    @pl.when(step == 0)
    def _():
        load.start()
        total[...] = jnp.zeros_like(total)
        mean_ref[...] = jnp.zeros_like(mean_ref)

    rows = emb_ref[...]
    mean_ref[...] += jnp.sum(rows.astype(f32), axis=0, keepdims=True)
    for at in range(0, width, tile):
        total[at : at + tile, at:] += dot(rows[:, at : at + tile], rows[:, at:], ((0,), (0,)))

    @pl.when(step == pl.num_programs(0) - 1)
    def _():
        share = 1.0 / (rows.shape[0] * pl.num_programs(0))
        mean = mean_ref[...] * share
        mean_ref[...] = mean
        load.wait()
        start = start_ref[...]
        start_top, start_low = split(start)
        mm = ((1,), (0,))
        down = [stand(mean[:, at : at + 128]) for at in range(0, width, 128)]
        along = weigh(down, start)
        for at in range(0, width, 128):
            for to in range(at // tile * tile, width, 128):
                block = total[at : at + 128, to : to + 128] * share
                block = block - down[at // 128] * mean[:, to : to + 128]
                cov_ref[at : at + 128, to : to + 128] = block
                if to // tile != at // tile:
                    cov_ref[to : to + 128, at : at + 128] = jnp.transpose(block)
        save.start()
        piece = width // devices
        for at in range(0, width, 128):
            top, low = split(cov_ref[at : at + 128, :])
            image = dot(top, start_top, mm) + dot(top, start_low, mm) + dot(low, start_top, mm)
            for half in range(n // 128):
                part = image[:, half * 128 : half * 128 + 128]
                part = part + down[at // 128] * along[:, half * 128 : half * 128 + 128]
                for sub in range(128 // piece):
                    image_ref[at // piece + sub, half * piece : half * piece + piece, :] = part[
                        sub * piece : sub * piece + piece
                    ]
        extra = n // 128 * piece
        for row in range(width // 128):
            image_ref[:, extra + row : extra + row + 1, :] = jnp.broadcast_to(
                mean[:, row * 128 : row * 128 + 128][None], (devices, 1, 128)
            )
        members = devices // 2
        keep_ref[...] = image_ref[pl.ds(side_ref[0] * members, members)]
        send_ref[...] = image_ref[pl.ds((1 - side_ref[0]) * members, members)]
        save.wait()


def moments(side, emb, start, devices):
    rows, width = emb.shape
    n = start.shape[1]
    tall = n // 128 * (width // devices) + width // 128
    half = (devices // 2, tall, 128)
    whole = lambda *shape: pl.BlockSpec(shape, lambda i, *_: (0,) * len(shape))
    return pl.pallas_call(
        functools.partial(moments_kernel, devices),
        grid_spec=pltpu.PrefetchScalarGridSpec(
            num_scalar_prefetch=1,
            grid=(STEPS,),
            in_specs=[pl.BlockSpec((rows // STEPS, width), lambda i, *_: (i, 0)), IN_HBM],
            out_specs=[IN_HBM, whole(*half), whole(*half), whole(1, width)],
            scratch_shapes=[
                pltpu.VMEM((width, width), f32),
                pltpu.VMEM((width, width), f32),
                pltpu.VMEM((width, n), f32),
                pltpu.VMEM((devices, tall, 128), f32),
                pltpu.SemaphoreType.DMA((2,)),
            ],
        ),
        out_shape=[
            jax.ShapeDtypeStruct((width, width), f32),
            jax.ShapeDtypeStruct(half, f32),
            jax.ShapeDtypeStruct(half, f32),
            jax.ShapeDtypeStruct((1, width), f32),
        ],
        compiler_params=grant("arbitrary", room=52),
        name="moments",
    )(side, emb, start)


def basis_kernel(
    devices, side_ref, mine_ref, other_ref, mean_ref, here_ref, start_ref, cov_hbm,
    basis_ref, flip_ref, eigen_ref, image_at, aug, cov_ref, turned, sem,
):
    load = pltpu.make_async_copy(cov_hbm, cov_ref, sem)
    load.start()
    width, n = start_ref.shape
    members, piece = mine_ref.shape[0], width // devices
    half = width // 2
    share = 1.0 / devices
    side = side_ref[0]
    for from_ref, at in ((mine_ref, side), (other_ref, 1 - side)):
        first = pl.multiple_of(at * half, half)
        for member in range(members):
            for part in range(n // 128):
                image_at[
                    pl.ds(first + member * piece, piece), part * 128 : part * 128 + 128
                ] = from_ref[member, part * piece : part * piece + piece, :]
    downs = [stand(mean_ref[row : row + 1, :]) for row in range(width // 128)]
    along = weigh(downs, start_ref)
    for row, down in enumerate(downs):
        at = slice(row * 128, row * 128 + 128)
        for part in range(0, n, 128):
            image_at[at, part : part + 128] = (
                image_at[at, part : part + 128] * share - down * along[:, part : part + 128]
            )
    image = image_at[...]
    aug[:, :n] = dot(image, image, ((0,), (0,)), HIGHEST)
    aug[:, n:] = (
        lax.broadcasted_iota(jnp.int32, (n, n), 0) == lax.broadcasted_iota(jnp.int32, (n, n), 1)
    ).astype(f32)
    eye = (
        lax.broadcasted_iota(jnp.int32, (PANEL, PANEL), 0)
        == lax.broadcasted_iota(jnp.int32, (PANEL, PANEL), 1)
    ).astype(f32)
    load.wait()
    cov_top, cov_low = split(cov_ref[...])
    image_top, image_low = split(image)
    mm = ((1,), (0,))
    turned[...] = (
        dot(cov_top, image_top, mm) + dot(cov_top, image_low, mm) + dot(cov_low, image_top, mm)
    )
    for first in range(0, n, PANEL):
        last = first + PANEL
        active = jnp.concatenate([aug[first:last, first:last], eye], axis=1)
        done = []
        for lead in range(0, PANEL, GROUP):
            row = lax.broadcasted_iota(jnp.int32, active.shape, 0)
            columns = [
                jnp.broadcast_to(active[:, lead + i : lead + i + 1], active.shape)
                for i in range(GROUP)
            ]
            pivots = [active[i : i + 1, :] for i in range(GROUP)]
            scale = jnp.zeros((GROUP, 2 * PANEL), f32)
            for i in range(GROUP):
                pivot = columns[i][i : i + 1, :]
                scale = jnp.where(row[:GROUP] == i, lax.rsqrt(pivot), scale)
                factor = jnp.where(row > i, columns[i] * (1.0 / pivot), 0.0)
                for j in range(i + 1, GROUP):
                    columns[j] = columns[j] - factor * columns[j][i : i + 1, :]
                for j in range(i + 1, GROUP):
                    pivots[j] = pivots[j] - factor[j : j + 1, :] * pivots[i]
                active = active - factor * pivots[i]
            done.append(active[:GROUP] * scale)
            active = active[GROUP:]
        inverse = jnp.concatenate(done, axis=0)[:, PANEL:]
        upper = dot(inverse, aug[first:last, :], ((1,), (0,)), HIGHEST)
        aug[first:last, :] = upper
        if last < n:
            aug[last:, :] = aug[last:, :] - dot(
                upper[:, last:n], upper, ((0,), (0,)), HIGHEST
            )
    basis = dot(image, aug[:, n:], ((1,), (1,)), HIGHEST)
    basis_ref[...] = basis
    turn_top, turn_low = split(aug[:, n:])
    turned_top, turned_low = split(turned[...])
    nt = ((1,), (1,))
    curved = dot(turned_top, turn_top, nt) + dot(turned_top, turn_low, nt) + dot(turned_low, turn_top, nt)
    eigen = jnp.sum(basis * curved, axis=0, keepdims=True)
    apart = weigh(
        [
            stand(here_ref[:, row * 128 : row * 128 + 128] - mean_ref[row : row + 1, :])
            for row in range(width // 128)
        ],
        basis,
    )
    eigen = (eigen + apart * apart) * share
    eigen_ref[...] = jnp.broadcast_to(eigen[None], eigen_ref.shape)
    signed = math.sqrt(width) * jnp.sum(basis, axis=0, keepdims=True)
    flip_ref[...] = signed / jnp.maximum(jnp.abs(signed), 1.0)


def basis_of(side, mine, other, mean, here, start, cov, devices):
    width, n = start.shape
    vmem = pl.BlockSpec(memory_space=pltpu.VMEM)
    return pl.pallas_call(
        functools.partial(basis_kernel, devices),
        in_specs=[pl.BlockSpec(memory_space=pltpu.SMEM)] + [vmem] * 5 + [IN_HBM],
        out_shape=(
            jax.ShapeDtypeStruct((width, n), f32),
            jax.ShapeDtypeStruct((1, n), f32),
            jax.ShapeDtypeStruct((devices, 1, n), f32),
        ),
        scratch_shapes=[
            pltpu.VMEM((width, n), f32),
            pltpu.VMEM((n, 2 * n), f32),
            pltpu.VMEM((width, width), f32),
            pltpu.VMEM((width, n), f32),
            pltpu.SemaphoreType.DMA(()),
        ],
        compiler_params=grant(room=48),
        name="basis",
    )(side, mine, other, mean, here, start, cov)


def route_kernel(
    owners, dest_ref, me_ref, emb_ref, noise_ref, basis_ref, flip_ref, eigen_ref, mean_ref, *refs
):
    outs, (whiten, offset, fresh, slot, ready, sems) = refs[:owners], refs[owners:]
    step = pl.program_id(0)
    n = basis_ref.shape[1]
    parts = n // 128

    @pl.when(step == 0)
    def _():
        eigen = jnp.sum(eigen_ref[...], axis=0)
        whiten[...] = (basis_ref[...] * (flip_ref[...] / jnp.sqrt(eigen + 1e-06))).astype(bf16)
        offset[...] = weigh(
            [stand(mean_ref[row : row + 1, :]) for row in range(mean_ref.shape[0])], whiten
        )

    values = dot(emb_ref[...], whiten[...], ((1,), (0,))) - offset[...] + noise_ref[...].astype(f32)
    for part in range(parts):
        fresh[part] = values[:, part * 128 : (part + 1) * 128]
    first = step * ROWS_STEP

    def move(group, carry):
        lead = group * MOVED
        ats = [dest_ref[first + lead + r] for r in range(MOVED)]
        for part in range(parts):
            rows = [fresh[part, pl.ds(lead + r, 1), :] for r in range(MOVED)]
            for at, row in zip(ats, rows):
                slot[part, pl.ds(at, 1), :] = row
        return carry

    lax.fori_loop(0, ROWS_STEP // MOVED, move, 0)

    @pl.when(step == pl.num_programs(0) - 1)
    def _():
        size, room = slot.shape[1] // owners, outs[0].shape[0]
        saves = [pltpu.make_async_copy(ready.at[k], outs[k], sems.at[k]) for k in range(owners)]
        for k in range(owners):
            at = pl.multiple_of(lax.rem(me_ref[0] + k, owners) * size, size)
            for part in range(parts):
                ready[k, :, part * 128 : (part + 1) * 128] = slot[part, pl.ds(at, room), :].astype(bf16)
            saves[k].start()
        for save in saves:
            save.wait()


def route(dest, me, emb, noise, basis, flip, eigen, mean, owners, slot_count, room):
    rows, width = emb.shape
    n = basis.shape[1]
    whole = lambda array: pl.BlockSpec(array.shape, lambda i, *_: (0,) * array.ndim)
    return pl.pallas_call(
        functools.partial(route_kernel, owners),
        grid_spec=pltpu.PrefetchScalarGridSpec(
            num_scalar_prefetch=2,
            grid=(rows // ROWS_STEP,),
            in_specs=[
                pl.BlockSpec((ROWS_STEP, width), lambda i, *_: (i, 0)),
                pl.BlockSpec((ROWS_STEP, n), lambda i, *_: (i, 0)),
                whole(basis), whole(flip), whole(eigen), whole(mean),
            ],
            out_specs=[pl.BlockSpec(memory_space=pl.ANY)] * owners,
            scratch_shapes=[
                pltpu.VMEM((width, n), bf16),
                pltpu.VMEM((1, n), f32),
                pltpu.VMEM((n // 128, ROWS_STEP, 128), f32),
                pltpu.VMEM((n // 128, slot_count, 128), f32),
                pltpu.VMEM((owners, room, n), bf16),
                pltpu.SemaphoreType.DMA((owners,)),
            ],
        ),
        out_shape=[jax.ShapeDtypeStruct((room, n), bf16)] * owners,
        compiler_params=grant("arbitrary"),
        name="route",
    )(dest, me, emb, noise, basis, flip, eigen, mean)


PART = 4


def unpack_kernel(capacity, source_ref, count_ref, block_ref, *refs):
    out_ref = refs[-1]
    lead = pl.program_id(0) * PART
    room, n = block_ref.shape
    base = source_ref[0] * CL_DEV
    tile = lax.fori_loop(
        0, lead, lambda c, at: at + (count_ref[base + c] + (TILE - 1)) // TILE, jnp.int32(0)
    )
    row = lax.broadcasted_iota(jnp.int32, (TILE, n), 0)
    for c in range(PART):
        count = count_ref[base + lead + c]
        for t in range(capacity // TILE):
            at = pl.multiple_of(jnp.minimum(tile + t, room // TILE - 1) * TILE, TILE)
            rows = block_ref[pl.ds(at, TILE), :]
            out_ref[c, 0, t * TILE : t * TILE + TILE, :] = jnp.where(
                row < count - t * TILE, rows, jnp.zeros_like(rows)
            )
        tile = tile + (count + (TILE - 1)) // TILE


def unpack(source, counts, block, arrived, owners, capacity):
    room, n = block.shape
    spec = pl.BlockSpec((PART, 1, capacity, n), lambda i, source_ref, *_: (i, source_ref[0], 0, 0))
    extra = [] if arrived is None else [arrived]
    return pl.pallas_call(
        functools.partial(unpack_kernel, capacity),
        grid_spec=pltpu.PrefetchScalarGridSpec(
            num_scalar_prefetch=2,
            grid=(CL_DEV // PART,),
            in_specs=[pl.BlockSpec((room, n), lambda i, *_: (0, 0))]
            + [pl.BlockSpec(memory_space=pl.ANY)] * len(extra),
            out_specs=spec,
        ),
        out_shape=jax.ShapeDtypeStruct((CL_DEV, owners, capacity, n), bf16),
        input_output_aliases={3: 0} if extra else {},
        compiler_params=grant("arbitrary"),
        cost_estimate=pl.CostEstimate(flops=1 << 20, bytes_accessed=1 << 20, transcendentals=0),
        name="unpack",
    )(source, counts, block, *extra)


def swap_pairs(block):
    return lax.ppermute(block, "dp", [(i, i ^ 1) for i in range(lax.axis_size("dp"))])


def exchange(blocks, groups=None):
    return lax.all_to_all(
        blocks, AXES, split_axis=0, concat_axis=0, tiled=True, axis_index_groups=groups
    )


def shards(embeddings, cluster_ids, noise, start_basis):
    rows_dev, width = embeddings.shape
    n = start_basis.shape[1]
    dp_size, owners = lax.axis_size("dp"), lax.axis_size("owner")
    devices = dp_size * owners
    clusters = CL_DEV * owners
    capacity = 2 * rows_dev // clusters
    place, count = slots(cluster_ids[:, 0], clusters, capacity)
    count = jnp.pad(count, ((0, 0), (0, -clusters % 128)))
    side = (lax.axis_index("dp") % 2).astype(jnp.int32)[None]
    covariance, keep, send, mean_here = moments(side, embeddings, start_basis, devices)

    groups = [
        [d * owners + o for d in range(side, dp_size, 2) for o in range(owners)]
        for side in range(2)
    ]
    members = devices // 2
    piece = jnp.sum(exchange(keep + swap_pairs(send), groups), axis=0)
    tall = piece.shape[0] - width // 128
    mean = piece[tall:] / devices
    sent = jnp.concatenate([piece[:tall], count])
    mine = exchange(jnp.broadcast_to(sent[None], (members,) + sent.shape), groups)
    other = swap_pairs(mine)

    basis, flip, eigen = basis_of(
        side, mine, other, mean, mean_here, start_basis, covariance, devices
    )
    me = lax.axis_index("owner").astype(jnp.int32)
    tables = [t[:, tall, :clusters].astype(jnp.int32) for t in (mine, other)]
    rooms = [level * (CL_DEV * capacity) // 64 for level in LEVELS]
    need = jnp.int32(0)
    for table in tables:
        tiles = (table + (TILE - 1)) // TILE * TILE
        need = jnp.maximum(need, jnp.max(jnp.sum(tiles.reshape(members, owners, CL_DEV), axis=2)))
    level = jnp.sum((need > jnp.array(rooms[:-1], jnp.int32)).astype(jnp.int32))
    row_of = lax.axis_index("dp") // 2 * owners
    counts = lax.dynamic_slice(tables[0], (row_of, me * CL_DEV), (owners, CL_DEV)).reshape(-1)

    def deliver(room, place, me, embeddings, noise, basis, flip, eigen, mean, counts):
        blocks = route(
            place, me[None], embeddings, noise, basis, flip, eigen, mean,
            owners, clusters * capacity, room,
        )
        arrived = None
        for step in range(owners):
            block = blocks[step]
            if step:
                block = lax.ppermute(
                    block, "owner", [(i, (i + step) % owners) for i in range(owners)]
                )
            source = (me - step + owners) % owners
            arrived = unpack(source[None], counts, block, arrived, owners, capacity)
        return arrived

    arrived = lax.switch(
        level,
        [functools.partial(deliver, room) for room in rooms],
        place, me, embeddings, noise, basis, flip, exchange(eigen), mean, counts,
    )
    return arrived[None]


def solution(mesh):
    return jax.shard_map(
        shards,
        mesh=mesh,
        in_specs=(P(AXES, None), P(AXES, None), P(AXES, None), P()),
        out_specs=P("dp", "owner", None, None, None),
        check_vma=False,
    )
```

```python
import functools
import math

import jax
import jax.numpy as jnp
from jax import lax
from jax.experimental import pallas as pl
from jax.experimental.pallas import tpu as pltpu
from jax.sharding import PartitionSpec as P

f32, bf16 = jnp.float32, jnp.bfloat16
HIGHEST = lax.Precision.HIGHEST
AXES = ("dp", "owner")
CL_DEV = 8
PANEL = 64
GROUP = 16
ROWS_STEP = 512
MOVED = 64
STEPS = 4
TILE = 8
LEVELS = (46, 49, 52, 56, 64)

IN_HBM = pl.BlockSpec(memory_space=pltpu.MemorySpace.HBM)


def dot(a, b, dims, precision=None):
    return lax.dot_general(a, b, (dims, ((), ())), precision=precision, preferred_element_type=f32)


def split(x):
    top = x.astype(bf16)
    return top, (x - top.astype(f32)).astype(bf16)


def stand(row):
    return jnp.transpose(jnp.broadcast_to(row, (128, 128)))


def weigh(downs, table):
    sums = []
    for part in range(0, table.shape[1], 128):
        total = jnp.zeros((128, 128), f32)
        for index, down in enumerate(downs):
            total = total + down * table[index * 128 : index * 128 + 128, part : part + 128].astype(f32)
        sums.append(jnp.sum(total, axis=0, keepdims=True))
    return jnp.concatenate(sums, axis=1)


def grant(*order, room=24):
    return pltpu.CompilerParams(vmem_limit_bytes=room << 20, dimension_semantics=order or None)


def slots_kernel(capacity, ids_ref, out_ref, count_ref):
    blocks, width = ids_ref.shape
    clusters = count_ref.shape[1]
    names = lax.broadcasted_iota(jnp.int32, (clusters, width), 0)
    above = (
        lax.broadcasted_iota(jnp.int32, (width, width), 0)
        < lax.broadcasted_iota(jnp.int32, (width, width), 1)
    ).astype(bf16)
    count = jnp.zeros((clusters, 1), f32)
    count_ref[...] = jnp.zeros_like(count_ref)
    for block in range(blocks):
        hit = (names == ids_ref[block : block + 1, :]).astype(f32)
        before = dot(hit.astype(bf16), above, ((1,), (0,))) + count
        out_ref[block : block + 1, :] = jnp.sum(hit * before, axis=0, keepdims=True).astype(jnp.int32)
        count_ref[...] += dot(jnp.ones((8, width), bf16), hit.astype(bf16), ((1,), (1,)))
        count = count + jnp.sum(hit, axis=1, keepdims=True)
    tiles = jnp.broadcast_to(((count.astype(jnp.int32) + (TILE - 1)) // TILE).astype(f32), (clusters, width))
    later = lax.broadcasted_iota(jnp.int32, (clusters, clusters), 0)
    early = lax.broadcasted_iota(jnp.int32, (clusters, clusters), 1)
    ahead = (early < later) & (early // CL_DEV == later // CL_DEV)
    start = dot(ahead.astype(bf16), tiles.astype(bf16), ((1,), (0,))) * TILE
    start = start + (names // CL_DEV * (CL_DEV * capacity)).astype(f32)
    for block in range(blocks):
        hit = names == ids_ref[block : block + 1, :]
        first = jnp.sum(jnp.where(hit, start, 0.0), axis=0, keepdims=True)
        out_ref[block : block + 1, :] += first.astype(jnp.int32)


def slots(ids, clusters, capacity):
    rows = ids.shape[0]
    place, count = pl.pallas_call(
        functools.partial(slots_kernel, capacity),
        out_shape=(
            jax.ShapeDtypeStruct((rows // 128, 128), jnp.int32),
            jax.ShapeDtypeStruct((8, clusters), f32),
        ),
        cost_estimate=pl.CostEstimate(flops=1 << 30, bytes_accessed=1 << 22, transcendentals=0),
        name="slots",
    )(ids.reshape(rows // 128, 128))
    return place.reshape(rows), count


def moments_kernel(
    devices, side_ref, emb_ref, start_hbm, cov_hbm, keep_ref, send_ref, mean_ref,
    total, cov_ref, start_ref, image_ref, sems,
):
    step = pl.program_id(0)
    width, n = start_ref.shape
    tile = min(256, width)
    load = pltpu.make_async_copy(start_hbm, start_ref, sems.at[0])
    save = pltpu.make_async_copy(cov_ref, cov_hbm, sems.at[1])

    @pl.when(step == 0)
    def _():
        load.start()
        total[...] = jnp.zeros_like(total)
        mean_ref[...] = jnp.zeros_like(mean_ref)

    rows = emb_ref[...]
    mean_ref[...] += jnp.sum(rows.astype(f32), axis=0, keepdims=True)
    for at in range(0, width, tile):
        total[at : at + tile, at:] += dot(rows[:, at : at + tile], rows[:, at:], ((0,), (0,)))

    @pl.when(step == pl.num_programs(0) - 1)
    def _():
        share = 1.0 / (rows.shape[0] * pl.num_programs(0))
        mean = mean_ref[...] * share
        mean_ref[...] = mean
        load.wait()
        start = start_ref[...]
        start_top, start_low = split(start)
        mm = ((1,), (0,))
        down = [stand(mean[:, at : at + 128]) for at in range(0, width, 128)]
        along = weigh(down, start)
        for at in range(0, width, 128):
            for to in range(at // tile * tile, width, 128):
                block = total[at : at + 128, to : to + 128] * share
                block = block - down[at // 128] * mean[:, to : to + 128]
                cov_ref[at : at + 128, to : to + 128] = block
                if to // tile != at // tile:
                    cov_ref[to : to + 128, at : at + 128] = jnp.transpose(block)
        save.start()
        piece = width // devices
        for at in range(0, width, 128):
            top, low = split(cov_ref[at : at + 128, :])
            image = dot(top, start_top, mm) + dot(top, start_low, mm) + dot(low, start_top, mm)
            for half in range(n // 128):
                part = image[:, half * 128 : half * 128 + 128]
                part = part + down[at // 128] * along[:, half * 128 : half * 128 + 128]
                for sub in range(128 // piece):
                    image_ref[at // piece + sub, half * piece : half * piece + piece, :] = part[
                        sub * piece : sub * piece + piece
                    ]
        extra = n // 128 * piece
        for row in range(width // 128):
            image_ref[:, extra + row : extra + row + 1, :] = jnp.broadcast_to(
                mean[:, row * 128 : row * 128 + 128][None], (devices, 1, 128)
            )
        members = devices // 2
        keep_ref[...] = image_ref[pl.ds(side_ref[0] * members, members)]
        send_ref[...] = image_ref[pl.ds((1 - side_ref[0]) * members, members)]
        save.wait()


def moments(side, emb, start, devices):
    rows, width = emb.shape
    n = start.shape[1]
    tall = n // 128 * (width // devices) + width // 128
    half = (devices // 2, tall, 128)
    whole = lambda *shape: pl.BlockSpec(shape, lambda i, *_: (0,) * len(shape))
    return pl.pallas_call(
        functools.partial(moments_kernel, devices),
        grid_spec=pltpu.PrefetchScalarGridSpec(
            num_scalar_prefetch=1,
            grid=(STEPS,),
            in_specs=[pl.BlockSpec((rows // STEPS, width), lambda i, *_: (i, 0)), IN_HBM],
            out_specs=[IN_HBM, whole(*half), whole(*half), whole(1, width)],
            scratch_shapes=[
                pltpu.VMEM((width, width), f32),
                pltpu.VMEM((width, width), f32),
                pltpu.VMEM((width, n), f32),
                pltpu.VMEM((devices, tall, 128), f32),
                pltpu.SemaphoreType.DMA((2,)),
            ],
        ),
        out_shape=[
            jax.ShapeDtypeStruct((width, width), f32),
            jax.ShapeDtypeStruct(half, f32),
            jax.ShapeDtypeStruct(half, f32),
            jax.ShapeDtypeStruct((1, width), f32),
        ],
        compiler_params=grant("arbitrary", room=52),
        name="moments",
    )(side, emb, start)


def basis_kernel(
    devices, side_ref, mine_ref, other_ref, mean_ref, here_ref, start_ref, cov_hbm,
    basis_ref, flip_ref, eigen_ref, image_at, aug, cov_ref, turned, sem,
):
    load = pltpu.make_async_copy(cov_hbm, cov_ref, sem)
    load.start()
    width, n = start_ref.shape
    members, piece = mine_ref.shape[0], width // devices
    half = width // 2
    share = 1.0 / devices
    side = side_ref[0]
    for from_ref, at in ((mine_ref, side), (other_ref, 1 - side)):
        first = pl.multiple_of(at * half, half)
        for member in range(members):
            for part in range(n // 128):
                image_at[
                    pl.ds(first + member * piece, piece), part * 128 : part * 128 + 128
                ] = from_ref[member, part * piece : part * piece + piece, :]
    downs = [stand(mean_ref[row : row + 1, :]) for row in range(width // 128)]
    along = weigh(downs, start_ref)
    for row, down in enumerate(downs):
        at = slice(row * 128, row * 128 + 128)
        for part in range(0, n, 128):
            image_at[at, part : part + 128] = (
                image_at[at, part : part + 128] * share - down * along[:, part : part + 128]
            )
    image = image_at[...]
    aug[:, :n] = dot(image, image, ((0,), (0,)), HIGHEST)
    aug[:, n:] = (
        lax.broadcasted_iota(jnp.int32, (n, n), 0) == lax.broadcasted_iota(jnp.int32, (n, n), 1)
    ).astype(f32)
    eye = (
        lax.broadcasted_iota(jnp.int32, (PANEL, PANEL), 0)
        == lax.broadcasted_iota(jnp.int32, (PANEL, PANEL), 1)
    ).astype(f32)
    load.wait()
    cov_top, cov_low = split(cov_ref[...])
    image_top, image_low = split(image)
    mm = ((1,), (0,))
    turned[...] = (
        dot(cov_top, image_top, mm) + dot(cov_top, image_low, mm) + dot(cov_low, image_top, mm)
    )
    for first in range(0, n, PANEL):
        last = first + PANEL
        active = jnp.concatenate([aug[first:last, first:last], eye], axis=1)
        done = []
        for lead in range(0, PANEL, GROUP):
            row = lax.broadcasted_iota(jnp.int32, active.shape, 0)
            columns = [
                jnp.broadcast_to(active[:, lead + i : lead + i + 1], active.shape)
                for i in range(GROUP)
            ]
            pivots = [active[i : i + 1, :] for i in range(GROUP)]
            scale = jnp.zeros((GROUP, 2 * PANEL), f32)
            for i in range(GROUP):
                pivot = columns[i][i : i + 1, :]
                scale = jnp.where(row[:GROUP] == i, lax.rsqrt(pivot), scale)
                factor = jnp.where(row > i, columns[i] * (1.0 / pivot), 0.0)
                for j in range(i + 1, GROUP):
                    columns[j] = columns[j] - factor * columns[j][i : i + 1, :]
                for j in range(i + 1, GROUP):
                    pivots[j] = pivots[j] - factor[j : j + 1, :] * pivots[i]
                active = active - factor * pivots[i]
            done.append(active[:GROUP] * scale)
            active = active[GROUP:]
        inverse = jnp.concatenate(done, axis=0)[:, PANEL:]
        upper = dot(inverse, aug[first:last, :], ((1,), (0,)), HIGHEST)
        aug[first:last, :] = upper
        if last < n:
            aug[last:, :] = aug[last:, :] - dot(
                upper[:, last:n], upper, ((0,), (0,)), HIGHEST
            )
    basis = dot(image, aug[:, n:], ((1,), (1,)), HIGHEST)
    basis_ref[...] = basis
    turn_top, turn_low = split(aug[:, n:])
    turned_top, turned_low = split(turned[...])
    nt = ((1,), (1,))
    curved = dot(turned_top, turn_top, nt) + dot(turned_top, turn_low, nt) + dot(turned_low, turn_top, nt)
    eigen = jnp.sum(basis * curved, axis=0, keepdims=True)
    apart = weigh(
        [
            stand(here_ref[:, row * 128 : row * 128 + 128] - mean_ref[row : row + 1, :])
            for row in range(width // 128)
        ],
        basis,
    )
    eigen = (eigen + apart * apart) * share
    eigen_ref[...] = jnp.broadcast_to(eigen[None], eigen_ref.shape)
    signed = math.sqrt(width) * jnp.sum(basis, axis=0, keepdims=True)
    flip_ref[...] = signed / jnp.maximum(jnp.abs(signed), 1.0)


def basis_of(side, mine, other, mean, here, start, cov, devices):
    width, n = start.shape
    vmem = pl.BlockSpec(memory_space=pltpu.VMEM)
    return pl.pallas_call(
        functools.partial(basis_kernel, devices),
        in_specs=[pl.BlockSpec(memory_space=pltpu.SMEM)] + [vmem] * 5 + [IN_HBM],
        out_shape=(
            jax.ShapeDtypeStruct((width, n), f32),
            jax.ShapeDtypeStruct((1, n), f32),
            jax.ShapeDtypeStruct((devices, 1, n), f32),
        ),
        scratch_shapes=[
            pltpu.VMEM((width, n), f32),
            pltpu.VMEM((n, 2 * n), f32),
            pltpu.VMEM((width, width), f32),
            pltpu.VMEM((width, n), f32),
            pltpu.SemaphoreType.DMA(()),
        ],
        compiler_params=grant(room=48),
        name="basis",
    )(side, mine, other, mean, here, start, cov)


def route_kernel(
    owners, dest_ref, me_ref, emb_ref, noise_ref, basis_ref, flip_ref, eigen_ref, mean_ref, *refs
):
    outs, (whiten, offset, fresh, slot, ready, sems) = refs[:owners], refs[owners:]
    step = pl.program_id(0)
    n = basis_ref.shape[1]
    parts = n // 128

    @pl.when(step == 0)
    def _():
        eigen = jnp.sum(eigen_ref[...], axis=0)
        whiten[...] = (basis_ref[...] * (flip_ref[...] / jnp.sqrt(eigen + 1e-06))).astype(bf16)
        offset[...] = weigh(
            [stand(mean_ref[row : row + 1, :]) for row in range(mean_ref.shape[0])], whiten
        )

    values = dot(emb_ref[...], whiten[...], ((1,), (0,))) - offset[...] + noise_ref[...].astype(f32)
    for part in range(parts):
        fresh[part] = values[:, part * 128 : (part + 1) * 128]
    first = step * ROWS_STEP

    def move(group, carry):
        lead = group * MOVED
        ats = [dest_ref[first + lead + r] for r in range(MOVED)]
        for part in range(parts):
            rows = [fresh[part, pl.ds(lead + r, 1), :] for r in range(MOVED)]
            for at, row in zip(ats, rows):
                slot[part, pl.ds(at, 1), :] = row
        return carry

    lax.fori_loop(0, ROWS_STEP // MOVED, move, 0)

    @pl.when(step == pl.num_programs(0) - 1)
    def _():
        size, room = slot.shape[1] // owners, outs[0].shape[0]
        saves = [pltpu.make_async_copy(ready.at[k], outs[k], sems.at[k]) for k in range(owners)]
        for k in range(owners):
            at = pl.multiple_of(lax.rem(me_ref[0] + k, owners) * size, size)
            for part in range(parts):
                ready[k, :, part * 128 : (part + 1) * 128] = slot[part, pl.ds(at, room), :].astype(bf16)
            saves[k].start()
        for save in saves:
            save.wait()


def route(dest, me, emb, noise, basis, flip, eigen, mean, owners, slot_count, room):
    rows, width = emb.shape
    n = basis.shape[1]
    whole = lambda array: pl.BlockSpec(array.shape, lambda i, *_: (0,) * array.ndim)
    return pl.pallas_call(
        functools.partial(route_kernel, owners),
        grid_spec=pltpu.PrefetchScalarGridSpec(
            num_scalar_prefetch=2,
            grid=(rows // ROWS_STEP,),
            in_specs=[
                pl.BlockSpec((ROWS_STEP, width), lambda i, *_: (i, 0)),
                pl.BlockSpec((ROWS_STEP, n), lambda i, *_: (i, 0)),
                whole(basis), whole(flip), whole(eigen), whole(mean),
            ],
            out_specs=[pl.BlockSpec(memory_space=pl.ANY)] * owners,
            scratch_shapes=[
                pltpu.VMEM((width, n), bf16),
                pltpu.VMEM((1, n), f32),
                pltpu.VMEM((n // 128, ROWS_STEP, 128), f32),
                pltpu.VMEM((n // 128, slot_count, 128), f32),
                pltpu.VMEM((owners, room, n), bf16),
                pltpu.SemaphoreType.DMA((owners,)),
            ],
        ),
        out_shape=[jax.ShapeDtypeStruct((room, n), bf16)] * owners,
        compiler_params=grant("arbitrary"),
        name="route",
    )(dest, me, emb, noise, basis, flip, eigen, mean)


PART = 4


def unpack_kernel(capacity, source_ref, count_ref, block_ref, *refs):
    out_ref = refs[-1]
    lead = pl.program_id(0) * PART
    room, n = block_ref.shape
    base = source_ref[0] * CL_DEV
    tile = lax.fori_loop(
        0, lead, lambda c, at: at + (count_ref[base + c] + (TILE - 1)) // TILE, jnp.int32(0)
    )
    row = lax.broadcasted_iota(jnp.int32, (TILE, n), 0)
    for c in range(PART):
        count = count_ref[base + lead + c]
        for t in range(capacity // TILE):
            at = pl.multiple_of(jnp.minimum(tile + t, room // TILE - 1) * TILE, TILE)
            rows = block_ref[pl.ds(at, TILE), :]
            out_ref[c, 0, t * TILE : t * TILE + TILE, :] = jnp.where(
                row < count - t * TILE, rows, jnp.zeros_like(rows)
            )
        tile = tile + (count + (TILE - 1)) // TILE


def unpack(source, counts, block, arrived, owners, capacity):
    room, n = block.shape
    spec = pl.BlockSpec((PART, 1, capacity, n), lambda i, source_ref, *_: (i, source_ref[0], 0, 0))
    extra = [] if arrived is None else [arrived]
    return pl.pallas_call(
        functools.partial(unpack_kernel, capacity),
        grid_spec=pltpu.PrefetchScalarGridSpec(
            num_scalar_prefetch=2,
            grid=(CL_DEV // PART,),
            in_specs=[pl.BlockSpec((room, n), lambda i, *_: (0, 0))]
            + [pl.BlockSpec(memory_space=pl.ANY)] * len(extra),
            out_specs=spec,
        ),
        out_shape=jax.ShapeDtypeStruct((CL_DEV, owners, capacity, n), bf16),
        input_output_aliases={3: 0} if extra else {},
        compiler_params=grant("arbitrary"),
        cost_estimate=pl.CostEstimate(flops=1 << 20, bytes_accessed=1 << 20, transcendentals=0),
        name="unpack",
    )(source, counts, block, *extra)


def swap_pairs(block):
    return lax.ppermute(block, "dp", [(i, i ^ 1) for i in range(lax.axis_size("dp"))])


def exchange(blocks, groups=None):
    return lax.all_to_all(
        blocks, AXES, split_axis=0, concat_axis=0, tiled=True, axis_index_groups=groups
    )


def shards(embeddings, cluster_ids, noise, start_basis):
    rows_dev, width = embeddings.shape
    n = start_basis.shape[1]
    dp_size, owners = lax.axis_size("dp"), lax.axis_size("owner")
    devices = dp_size * owners
    clusters = CL_DEV * owners
    capacity = 2 * rows_dev // clusters
    place, count = slots(cluster_ids[:, 0], clusters, capacity)
    count = jnp.pad(count, ((0, 0), (0, -clusters % 128)))
    side = (lax.axis_index("dp") % 2).astype(jnp.int32)[None]
    covariance, keep, send, mean_here = moments(side, embeddings, start_basis, devices)

    groups = [
        [d * owners + o for d in range(side, dp_size, 2) for o in range(owners)]
        for side in range(2)
    ]
    members = devices // 2
    piece = jnp.sum(exchange(keep + swap_pairs(send), groups), axis=0)
    tall = piece.shape[0] - width // 128
    mean = piece[tall:] / devices
    sent = jnp.concatenate([piece[:tall], count])
    mine = exchange(jnp.broadcast_to(sent[None], (members,) + sent.shape), groups)
    other = swap_pairs(mine)

    basis, flip, eigen = basis_of(
        side, mine, other, mean, mean_here, start_basis, covariance, devices
    )
    me = lax.axis_index("owner").astype(jnp.int32)
    tables = [t[:, tall, :clusters].astype(jnp.int32) for t in (mine, other)]
    rooms = [level * (CL_DEV * capacity) // 64 for level in LEVELS]
    need = jnp.int32(0)
    for table in tables:
        tiles = (table + (TILE - 1)) // TILE * TILE
        need = jnp.maximum(need, jnp.max(jnp.sum(tiles.reshape(members, owners, CL_DEV), axis=2)))
    level = jnp.sum((need > jnp.array(rooms[:-1], jnp.int32)).astype(jnp.int32))
    row_of = lax.axis_index("dp") // 2 * owners
    counts = lax.dynamic_slice(tables[0], (row_of, me * CL_DEV), (owners, CL_DEV)).reshape(-1)

    def deliver(room, place, me, embeddings, noise, basis, flip, eigen, mean, counts):
        blocks = route(
            place, me[None], embeddings, noise, basis, flip, eigen, mean,
            owners, clusters * capacity, room,
        )
        arrived = None
        for step in range(owners):
            block = blocks[step]
            if step:
                block = lax.ppermute(
                    block, "owner", [(i, (i + step) % owners) for i in range(owners)]
                )
            source = (me - step + owners) % owners
            arrived = unpack(source[None], counts, block, arrived, owners, capacity)
        return arrived

    arrived = lax.switch(
        level,
        [functools.partial(deliver, room) for room in rooms],
        place, me, embeddings, noise, basis, flip, exchange(eigen), mean, counts,
    )
    return arrived[None]


def solution(mesh):
    return jax.shard_map(
        shards,
        mesh=mesh,
        in_specs=(P(AXES, None), P(AXES, None), P(AXES, None), P()),
        out_specs=P("dp", "owner", None, None, None),
        check_vma=False,
    )
```
